512 devices in a mesh: gx: 4 (over x), gy: 16 (over z, core), gz: 8 (over y).
Axes of the slice: x: 4, y: 8, z: 8, core: 2. Of those that a mesh axis runs over, the one named last changes fastest.
Arguments:
- field: float32 [2, 128, 256, 2048], P(None, 'gz', 'gx', 'gy'), may hold values from -30 to 30
- transfer: float32 [4, 128], replicated, may hold values from 0.2 to 3
- light_angles: float32 [2], replicated, may hold values from -3.140625 to 3.140625
Outputs:
- image: float32 [4, 256, 2048], P(None, ('gx', 'gz'), 'gy')
The draws below stay inside these ranges and needn't reach their ends.
All inputs are finite; a program needn't handle non-finite values.
Results may differ from the reference program's by a relative error of at most 0.00019.
Values sent between devices are 32-bit elements; how exact they have to be, the bound alone decides.
No kernel may reach another device: no remote copies, remote signals or barrier semaphores. Data moves between devices by JAX's collectives and lax.ppermute only.
A program may use at most 64 MiB of HBM per device.

```python
import math
import jax
import jax.numpy as jnp
from jax import lax

BINS = 128
NX = 256
NY = 2048
NZ = 128


def draw_field(key, part):
    shape = (2, NZ, NX, NY)
    values = jax.random.normal(key, shape, jnp.float32) * 6.0
    return jnp.clip(values, -30.0, 30.0)


def setup_inputs(seed: int = 0) -> dict:
    arg_keys = jax.random.split(jax.random.key(seed), 4)
    field = draw_field(jax.random.fold_in(arg_keys[3], 71), 0)
    transfer = jnp.clip(jax.random.uniform(arg_keys[1], (4, BINS), jnp.float32, 0.2, 3.0), 0.2, 3.0)
    light_angles = jnp.clip(jax.random.uniform(arg_keys[2], (2,), jnp.float32, -3.140625, 3.140625), -3.140625, 3.140625)
    return dict(field=field, transfer=transfer, light_angles=light_angles)


SIGMA_TAPS = 1.2
OPTICAL = 2.0
SHADE_FLOOR = 0.25


def filter_taps():
    places = [-3, -2, -1, 0, 1, 2, 3]
    bell = [math.exp(-place * place / (2.0 * SIGMA_TAPS * SIGMA_TAPS)) for place in places]
    bell_total = sum(bell)
    slope_total = sum(place * place * weight for place, weight in zip(places, bell))
    smooth_taps = [weight / bell_total for weight in bell]
    slope_taps = [place * weight / slope_total for place, weight in zip(places, bell)]
    return smooth_taps, slope_taps


def sweep(volume, taps, axis_dim):
    length = volume.shape[axis_dim] - 6
    total = taps[0] * lax.slice_in_dim(volume, 0, length, axis=axis_dim)
    for place in range(1, 7):
        total = total + taps[place] * lax.slice_in_dim(volume, place, place + length, axis=axis_dim)
    return total


def depth_section(first, second):
    smooth_taps, slope_taps = filter_taps()
    return sweep(first, smooth_taps, 0), sweep(first, slope_taps, 0), sweep(second, smooth_taps, 0)


def cross_section(plain, slope, other):
    smooth_taps, slope_taps = filter_taps()
    return (sweep(plain, smooth_taps, 1), sweep(plain, slope_taps, 1),
            sweep(slope, smooth_taps, 1), sweep(other, smooth_taps, 1))


def row_section(plain, cross_slope, depth_slope, other):
    smooth_taps, slope_taps = filter_taps()
    value = sweep(plain, smooth_taps, 2)
    grad_y = sweep(plain, slope_taps, 2)
    grad_x = sweep(cross_slope, smooth_taps, 2)
    grad_z = sweep(depth_slope, smooth_taps, 2)
    mixture = sweep(other, smooth_taps, 2)
    return value, mixture, grad_x, grad_y, grad_z


def sample_plane(value, mixture, grad_x, grad_y, grad_z, transfer, light_angles, depth_step):
    bins = transfer.shape[1]
    position = jax.nn.sigmoid(value) * (bins - 1)
    centers = jnp.arange(bins).astype(position.dtype)
    tent = jnp.maximum(0.0, 1.0 - jnp.abs(position[None] - centers[:, None, None]))
    looked = jnp.einsum("cb,bxy->cxy", transfer, tent, precision=lax.Precision.HIGHEST)
    light_x = jnp.cos(light_angles[0]) * jnp.sin(light_angles[1])
    light_y = jnp.sin(light_angles[0]) * jnp.sin(light_angles[1])
    light_z = jnp.cos(light_angles[1])
    facing = grad_x * light_x + grad_y * light_y + grad_z * light_z
    diffuse = facing * facing / (grad_x * grad_x + grad_y * grad_y + grad_z * grad_z + SHADE_FLOOR)
    shade = 0.25 + 0.75 * diffuse
    alpha = 1.0 - jnp.exp(-OPTICAL * looked[3] * jax.nn.sigmoid(mixture) * depth_step)
    return jnp.concatenate([(alpha * shade)[None] * looked[:3], alpha[None]], 0)


def over(front, back):
    return front + (1.0 - front[3:4]) * back


def integrate(value, mixture, grad_x, grad_y, grad_z, transfer, light_angles, depth_step):
    def advance(running, planes):
        sample = sample_plane(planes[0], planes[1], planes[2], planes[3], planes[4],
                              transfer, light_angles, depth_step)
        return over(running, sample), None

    start = jnp.zeros((4,) + value.shape[1:], value.dtype)
    result, unused = lax.scan(advance, start, (value, mixture, grad_x, grad_y, grad_z))
    return result


def reference(field, transfer, light_angles):
    padded = jnp.pad(field, ((0, 0), (3, 3), (3, 3), (3, 3)))
    plain, slope, other = depth_section(padded[0], padded[1])
    cross_plain, cross_slope, depth_slope, cross_other = cross_section(plain, slope, other)
    value, mixture, grad_x, grad_y, grad_z = row_section(cross_plain, cross_slope, depth_slope, cross_other)
    return integrate(value, mixture, grad_x, grad_y, grad_z, transfer, light_angles, 1.0 / NZ)
```

```python
import math

import jax
import jax.numpy as jnp
import numpy as np
from jax import lax
from jax.experimental import pallas as pl
from jax.experimental.pallas import tpu as pltpu
from jax.sharding import PartitionSpec as P

SIGMA_TAPS = 1.2
OPTICAL = 2.0
SHADE_FLOOR = 0.25
F32 = jnp.float32


def filter_taps():
    places = [-3, -2, -1, 0, 1, 2, 3]
    bell = [math.exp(-place * place / (2.0 * SIGMA_TAPS * SIGMA_TAPS)) for place in places]
    bell_total = sum(bell)
    slope_total = sum((place * place * weight for place, weight in zip(places, bell)))
    smooth_taps = [weight / bell_total for weight in bell]
    slope_taps = [place * weight / slope_total for place, weight in zip(places, bell)]
    return (smooth_taps, slope_taps)


SMOOTH, SLOPE = filter_taps()


def smooth7(v):
    return (
        SMOOTH[3] * v[3]
        + SMOOTH[4] * (v[2] + v[4])
        + SMOOTH[5] * (v[1] + v[5])
        + SMOOTH[6] * (v[0] + v[6])
    )


def slope7(v):
    return SLOPE[4] * (v[4] - v[2]) + SLOPE[5] * (v[5] - v[1]) + SLOPE[6] * (v[6] - v[0])


def row_matrix():
    cells = np.full(256, 10**6)
    cells[:128] = np.arange(128)
    cells[128:131] = np.arange(-3, 0)
    cells[132:135] = np.arange(128, 131)
    matrix = np.zeros((256, 256), np.float64)
    for j in range(128):
        for o in range(-3, 4):
            k = np.nonzero(cells == j + o)[0][0]
            matrix[k, j] = SMOOTH[o + 3]
            matrix[k, 128 + j] = SLOPE[o + 3]
    return matrix.astype(np.float32)


def depth_kernel(field, before, after, out, low, high):
    def tile(r, carry):
        at = pl.multiple_of(r * 8, 8)

        def plane(f, d):
            if d < 0:
                return before[pl.ds(f * 192 + (d + 3) * 64 + at, 8), :]
            if d > 15:
                return after[pl.ds(f * 192 + (d - 16) * 64 + at, 8), :]
            return field[pl.ds(f * 1024 + d * 64 + at, 8), :]

        first = [plane(0, d) for d in range(-3, 19)]
        for d in range(16):
            out[pl.ds(d * 64 + at, 8), :] = smooth7(first[d : d + 7])
            out[pl.ds(1024 + d * 64 + at, 8), :] = slope7(first[d : d + 7])
        second = [plane(1, d) for d in range(-3, 19)]
        for d in range(16):
            out[pl.ds(2048 + d * 64 + at, 8), :] = smooth7(second[d : d + 7])
        return carry

    lax.fori_loop(0, 8, tile, 0)
    for j in range(3):
        for f in range(3):
            low[pl.ds(j * 48 + f * 16, 16), :] = out[pl.ds(f * 1024 + j, 16, stride=64), :]
            high[pl.ds(j * 48 + f * 16, 16), :] = out[pl.ds(f * 1024 + 61 + j, 16, stride=64), :]


def cross_kernel(source, before, after, out, up, down, edge):
    lane = lax.broadcasted_iota(jnp.int32, (8, 128), 1)
    slot = lane // 8
    firsthalf = lane % 8 < 4

    def quad(q, carry):
        packed = [[jnp.zeros((8, 128), F32)] * 2 for _ in range(4)]
        for dd in range(4):
            for f in range(3):
                base = pl.multiple_of(f * 1024 + q * 256 + dd * 64, 64)
                at = f * 16 + q * 4 + dd
                e = (dd * 3 + f) * 48
                edge[e + 5 : e + 8, :] = before[pl.ds(at, 3, stride=48), :]
                edge[e + 8 : e + 24, :] = source[pl.ds(base, 16), :]
                edge[e + 24 : e + 40, :] = source[pl.ds(base + 48, 16), :]
                edge[e + 40 : e + 43, :] = after[pl.ds(at, 3, stride=48), :]
                for r in range(8):
                    if r == 0:
                        v = [edge[e + 5 + k : e + 13 + k, :] for k in range(7)]
                    elif r == 7:
                        v = [edge[e + 29 + k : e + 37 + k, :] for k in range(7)]
                    else:
                        v = [source[pl.ds(base + r * 8 - 3 + k, 8), :] for k in range(7)]
                    results = [(0, smooth7(v)), (1, slope7(v))] if f == 0 else [(f + 1, smooth7(v))]
                    s = (dd % 2) * 8 + r
                    for g, value in results:
                        out[pl.ds(g * 1024 + q * 256 + dd * 64 + r * 8, 8), :] = value
                        moved = pltpu.roll(value, (8 * s + 3) % 128, 1)
                        packed[g][dd // 2] = jnp.where(slot == s, moved, packed[g][dd // 2])
        for g in range(4):
            a, b = packed[g]
            at = pl.ds(pl.multiple_of(g * 32 + q * 8, 8), 8)
            up[at, :] = jnp.where(firsthalf, a, pltpu.roll(b, 4, 1))
            down[at, :] = jnp.where(firsthalf, pltpu.roll(a, 125, 1), pltpu.roll(b, 1, 1))
        return carry

    lax.fori_loop(0, 4, quad, 0)


def sample_kernel(light, source, left, right, matrix, transfer, out, rows):
    lane = lax.broadcasted_iota(jnp.int32, (8, 128), 1)
    firsthalf = lane % 8 < 4

    def chunk(q, carry):
        for g in range(4):
            at = pl.ds(pl.multiple_of(g * 32 + q * 8, 8), 8)
            a = left[at, :]
            b = right[at, :]
            halves = (
                jnp.where(firsthalf, a, pltpu.roll(b, 4, 1)),
                jnp.where(firsthalf, pltpu.roll(a, 124, 1), b),
            )
            for h in range(2):
                base = pl.multiple_of(g * 1024 + q * 256 + h * 128, 128)
                halo = jnp.concatenate(
                    [pltpu.roll(halves[h], (128 - 8 * s) % 128, 1) for s in range(16)], axis=0
                )
                cells = jnp.concatenate([source[pl.ds(base, 128), :], halo], axis=1)
                weights = matrix[...] if g == 0 else matrix[:, 0:128]
                result = jnp.dot(
                    cells, weights, precision=lax.Precision.HIGHEST, preferred_element_type=F32
                )
                rows[pl.ds(base, 128), :] = result[:, 0:128]
                if g == 0:
                    rows[pl.ds(4096 + q * 256 + h * 128, 128), :] = result[:, 128:256]
        return carry

    lax.fori_loop(0, 4, chunk, 0)

    bins = 128
    table = [jnp.broadcast_to(transfer[c : c + 1, :], (8, bins)) for c in range(4)]
    rise = [
        jnp.where(lane < bins - 1, pltpu.roll(t, bins - 1, 1) - t, 0.0) for t in table
    ]
    light_x, light_y, light_z = light[0], light[1], light[2]
    depth_step = light[3]

    def tile(r, carry):
        total = [jnp.zeros((8, 128), F32)] * 3
        through = jnp.ones((8, 128), F32)
        for d in range(16):
            at = pl.multiple_of(d * 64 + r * 8, 8)
            value = rows[pl.ds(at, 8), :]
            grad_x = rows[pl.ds(1024 + at, 8), :]
            grad_z = rows[pl.ds(2048 + at, 8), :]
            mixture = rows[pl.ds(3072 + at, 8), :]
            grad_y = rows[pl.ds(4096 + at, 8), :]
            position = jax.nn.sigmoid(value) * (bins - 1)
            whole = jnp.floor(position)
            part = position - whole
            index = whole.astype(jnp.int32)
            looked = [
                jnp.take_along_axis(table[c], index, axis=1, mode="promise_in_bounds")
                + part * jnp.take_along_axis(rise[c], index, axis=1, mode="promise_in_bounds")
                for c in range(4)
            ]
            facing = grad_x * light_x + grad_y * light_y + grad_z * light_z
            diffuse = (
                facing
                * facing
                / (grad_x * grad_x + grad_y * grad_y + grad_z * grad_z + SHADE_FLOOR)
            )
            shade = 0.25 + 0.75 * diffuse
            alpha = 1.0 - jnp.exp(-OPTICAL * looked[3] * jax.nn.sigmoid(mixture) * depth_step)
            covered = through * alpha
            shaded = covered * shade
            for c in range(3):
                total[c] = total[c] + shaded * looked[c]
            through = through - covered
        at = pl.multiple_of(r * 32, 32)
        for c in range(3):
            out[pl.ds(at + c * 8, 8), :] = total[c]
        out[pl.ds(at + 24, 8), :] = 1.0 - through
        return carry

    lax.fori_loop(0, 8, tile, 0)


def over_kernel(pieces, out):
    total = [pieces[pl.ds(c * 8, 8), :] for c in range(4)]
    for k in range(1, 8):
        through = 1.0 - total[3]
        for c in range(4):
            total[c] = total[c] + through * pieces[pl.ds(k * 32 + c * 8, 8), :]
    for c in range(4):
        out[pl.ds(c * 8, 8), :] = total[c]


def vmem():
    return pl.BlockSpec(memory_space=pltpu.VMEM)


def call(kernel, name, args, outs, scratch=(), smem=0):
    return pl.pallas_call(
        kernel,
        name=name,
        out_shape=[jax.ShapeDtypeStruct(shape, F32) for shape in outs],
        in_specs=[pl.BlockSpec(memory_space=pltpu.SMEM)] * smem + [vmem()] * (len(args) - smem),
        out_specs=[vmem()] * len(outs),
        scratch_shapes=[pltpu.VMEM(shape, F32) for shape in scratch],
    )(*args)


def swap(to_next, to_previous, axis):
    size = lax.axis_size(axis)
    up = [(i, i + 1) for i in range(size - 1)]
    down = [(j, i) for i, j in up]
    return lax.ppermute(to_next, axis, up), lax.ppermute(to_previous, axis, down)


def shards(field, transfer, light_angles):
    depth_count = lax.axis_size("gz")
    depth_step = 1.0 / (field.shape[1] * depth_count)
    light = jnp.stack(
        [
            jnp.cos(light_angles[0]) * jnp.sin(light_angles[1]),
            jnp.sin(light_angles[0]) * jnp.sin(light_angles[1]),
            jnp.cos(light_angles[1]),
            jnp.asarray(depth_step, F32),
        ]
    )
    before, after = swap(field[:, 13:], field[:, :3], "gz")
    depth, low, high = call(
        depth_kernel,
        "depth",
        (field.reshape(2048, 128), before.reshape(384, 128), after.reshape(384, 128)),
        ((3072, 128), (144, 128), (144, 128)),
    )
    before, after = swap(high, low, "gx")
    cross, to_next, to_previous = call(
        cross_kernel,
        "cross",
        (depth, before, after),
        ((4096, 128), (128, 128), (128, 128)),
        ((576, 128),),
    )
    left, right = swap(to_next, to_previous, "gy")
    (partial_value,) = call(
        sample_kernel,
        "sample",
        (light, cross, left, right, jnp.asarray(row_matrix()), transfer),
        ((256, 128),),
        ((5120, 128),),
        1,
    )
    pieces = lax.all_to_all(partial_value.reshape(8, 32, 128), "gz", 0, 0)
    (image,) = call(over_kernel, "over", (pieces.reshape(256, 128),), ((32, 128),))
    return image.reshape(4, 8, 128)


def solution(mesh):
    placed = (P(None, "gz", "gx", "gy"), P(), P())
    return jax.shard_map(
        shards, mesh=mesh, in_specs=placed, out_specs=P(None, ("gx", "gz"), "gy"), check_vma=False
    )
```

```python
import functools
import math

import jax
import jax.numpy as jnp
import numpy as np
from jax import lax
from jax.experimental import pallas as pl
from jax.experimental.pallas import tpu as pltpu
from jax.sharding import PartitionSpec as P

SIGMA_TAPS = 1.2
OPTICAL = 2.0
SHADE_FLOOR = 0.25
F32 = jnp.float32
BF16 = jnp.bfloat16


def filter_taps():
    places = [-3, -2, -1, 0, 1, 2, 3]
    bell = [math.exp(-place * place / (2.0 * SIGMA_TAPS * SIGMA_TAPS)) for place in places]
    bell_total = sum(bell)
    slope_total = sum((place * place * weight for place, weight in zip(places, bell)))
    smooth_taps = [weight / bell_total for weight in bell]
    slope_taps = [place * weight / slope_total for place, weight in zip(places, bell)]
    return (smooth_taps, slope_taps)


SMOOTH, SLOPE = filter_taps()


def smooth7(v):
    return (
        SMOOTH[3] * v[3]
        + SMOOTH[4] * (v[2] + v[4])
        + SMOOTH[5] * (v[1] + v[5])
        + SMOOTH[6] * (v[0] + v[6])
    )


def slope7(v):
    return SLOPE[4] * (v[4] - v[2]) + SLOPE[5] * (v[5] - v[1]) + SLOPE[6] * (v[6] - v[0])


def faces_kernel(field, to_inner, to_outer):
    even_z = even("gz")
    for f in range(2):
        for k in range(0, 192, 64):
            low = field[pl.ds(f * 1024 + k, 64), :]
            high = field[pl.ds(f * 1024 + 832 + k, 64), :]
            to_inner[pl.ds(f * 192 + k, 64), :] = jnp.where(even_z, high, low)
            to_outer[pl.ds(f * 192 + k, 64), :] = jnp.where(even_z, low, high)


def depth_kernel(field, inner, outer, out, to_inner, to_outer):
    even_z = even("gz")
    even_x = even("gx")

    def tile(r, carry):
        at = pl.multiple_of(r * 8, 8)

        def plane(f, d):
            if d < 0:
                rows = pl.ds(f * 192 + (d + 3) * 64 + at, 8)
                return jnp.where(even_z, outer[rows, :], inner[rows, :])
            if d > 15:
                rows = pl.ds(f * 192 + (d - 16) * 64 + at, 8)
                return jnp.where(even_z, inner[rows, :], outer[rows, :])
            return field[pl.ds(f * 1024 + d * 64 + at, 8), :]

        first = [plane(0, d) for d in range(-3, 19)]
        for d in range(16):
            out[pl.ds(d * 64 + at, 8), :] = smooth7(first[d : d + 7])
            out[pl.ds(1024 + d * 64 + at, 8), :] = slope7(first[d : d + 7])
        second = [plane(1, d) for d in range(-3, 19)]
        for d in range(16):
            out[pl.ds(2048 + d * 64 + at, 8), :] = smooth7(second[d : d + 7])
        return carry

    lax.fori_loop(0, 8, tile, 0)
    for j in range(3):
        for f in range(3):
            low = out[pl.ds(f * 1024 + j, 16, stride=64), :]
            high = out[pl.ds(f * 1024 + 61 + j, 16, stride=64), :]
            to_inner[pl.ds(j * 48 + f * 16, 16), :] = jnp.where(even_x, high, low)
            to_outer[pl.ds(j * 48 + f * 16, 16), :] = jnp.where(even_x, low, high)


def cross_kernel(source, inner, outer, out, to_inner, to_outer, edge):
    even_x = even("gx")
    even_y = even("gy")
    lane = lax.broadcasted_iota(jnp.int32, (8, 128), 1)
    slot = lane // 8
    firsthalf = lane % 8 < 3
    packed = [[jnp.zeros((8, 128), F32)] * 8 for _ in range(4)]
    for f in range(3):
        for d in range(16):
            at = f * 16 + d
            base = at * 64
            e = at * 48
            a = inner[pl.ds(at, 3, stride=48), :]
            b = outer[pl.ds(at, 3, stride=48), :]
            edge[e + 5 : e + 8, :] = jnp.where(even_x, b, a)
            edge[e + 8 : e + 24, :] = source[base : base + 16, :]
            edge[e + 24 : e + 40, :] = source[base + 48 : base + 64, :]
            edge[e + 40 : e + 43, :] = jnp.where(even_x, a, b)
            for r in range(8):
                if r == 0:
                    v = [edge[e + 5 + k : e + 13 + k, :] for k in range(7)]
                elif r == 7:
                    v = [edge[e + 29 + k : e + 37 + k, :] for k in range(7)]
                else:
                    v = [source[base + r * 8 - 3 + k : base + r * 8 + 5 + k, :] for k in range(7)]
                results = [(0, smooth7(v)), (1, slope7(v))] if f == 0 else [(f + 1, smooth7(v))]
                for g, value in results:
                    row = g * 1024 + d * 64 + r * 8
                    out[row : row + 8, :] = value
                    moved = pltpu.roll(value, (8 * d + 3) % 128, 1)
                    packed[g][r] = jnp.where(slot == d, moved, packed[g][r])
        for g in ((0, 1) if f == 0 else (f + 1,)):
            for q in range(4):
                a, b = packed[g][2 * q : 2 * q + 2]
                at = g * 32 + q * 8
                up = jnp.where(firsthalf, a, pltpu.roll(b, 3, 1))
                down = jnp.where(firsthalf, pltpu.roll(a, 125, 1), b)
                to_inner[at : at + 8, :] = jnp.where(even_y, up, down)
                to_outer[at : at + 8, :] = jnp.where(even_y, down, up)


def lanes_from(value, offset):
    return pltpu.roll(value, -offset % 128, 1)


def parts(value):
    high = value.astype(BF16)
    rest = value - high.astype(F32)
    middle = rest.astype(BF16)
    return high, middle, (rest - middle.astype(F32)).astype(BF16)


def row_matrix():
    matrix = np.zeros((128, 256), np.float64)
    for j in range(128):
        for o in range(-3, 4):
            if 0 <= j + o < 128:
                matrix[j + o, j] = SMOOTH[o + 3]
                matrix[j + o, 128 + j] = SLOPE[o + 3]
    pieces = []
    rest = matrix.astype(np.float32)
    for _ in range(3):
        pieces.append(rest.astype(jnp.bfloat16))
        rest = rest - pieces[-1].astype(np.float32)
    return np.concatenate([pieces[k] for k in (0, 0, 1, 1, 0, 2)], axis=0)


def row_kernel(angles, source, matrix, out, light):
    azimuth = jnp.full((8, 128), angles[0])
    polar = jnp.full((8, 128), angles[1])
    light[0:8, :] = jnp.cos(azimuth) * jnp.sin(polar)
    light[8:16, :] = jnp.sin(azimuth) * jnp.sin(polar)
    light[16:24, :] = jnp.cos(polar)

    def filtered(at, weights):
        high, middle, low = parts(source[at, :])
        cells = jnp.concatenate([high, middle, high, middle, low, high], axis=1)
        return jnp.dot(cells, weights, preferred_element_type=F32)

    both = filtered(pl.ds(0, 1024), matrix[...])
    out[0:1024, :] = both[:, 0:128]
    out[4096:5120, :] = both[:, 128:256]

    def rest(i, carry):
        at = pl.ds(pl.multiple_of(1024 + i * 1024, 1024), 1024)
        out[at, :] = filtered(at, matrix[:, 0:128])
        return carry

    lax.fori_loop(0, 3, rest, 0)


def edge_matrix():
    matrix = np.zeros((256, 512), np.float32)
    for d in range(16):
        for h in range(2):
            for lane in range(6):
                for o in (-3, -2, -1, 1, 2, 3):
                    cell = lane + o
                    if 0 <= cell < 6 and (lane < 3) == (o > 0) and (lane < 3) != (cell < 3):
                        row = 8 * d + 3 * h + cell % 3 + (128 if cell >= 3 else 0)
                        column = 256 * h + 8 * d + lane
                        matrix[row, column] = SMOOTH[o + 3]
                        matrix[row, column + 128] = SLOPE[o + 3]
    return matrix


def sample_kernel(light, source, inner, outer, matrix, transfer, out, grids, *, scale):
    even_y = even("gy")
    lane = lax.broadcasted_iota(jnp.int32, (8, 128), 1)
    outermost = (lane < 3) | (lane >= 125)

    left = jnp.where(even_y, outer[...], inner[...])
    right = jnp.where(even_y, inner[...], outer[...])
    terms = jnp.dot(
        jnp.concatenate([left, right], axis=1),
        matrix[...],
        precision=lax.Precision.HIGHEST,
        preferred_element_type=F32,
    )
    for g in range(5):
        for r in range(8):
            row = (g % 4) * 32 + (r // 2) * 8
            column = (r % 2) * 256 + (128 if g == 4 else 0)
            term = terms[row : row + 8, column : column + 128]
            for d in range(16):
                at = g * 1024 + d * 64 + r * 8
                moved = lanes_from(term, 8 * d + 3)
                grids[at : at + 8, :] = source[at : at + 8, :] + jnp.where(outermost, moved, 0.0)

    bins = 128
    table = [jnp.broadcast_to(transfer[c : c + 1, :], (8, bins)) for c in range(4)]
    rise = [jnp.where(lane < bins - 1, lanes_from(t, 1) - t, 0.0) for t in table]
    light_x, light_y, light_z = light[0:8, :], light[8:16, :], light[16:24, :]
    def tile(r, carry):
        total = [jnp.zeros((8, 128), F32)] * 3
        through = jnp.ones((8, 128), F32)
        for d in range(16):
            at = pl.multiple_of(d * 64 + r * 8, 8)
            value, grad_x, grad_z, mixture, grad_y = [
                grids[pl.ds(g * 1024 + at, 8), :] for g in range(5)
            ]
            position = jax.nn.sigmoid(value) * (bins - 1)
            whole = jnp.floor(position)
            part = position - whole
            index = whole.astype(jnp.int32)
            looked = [
                jnp.take_along_axis(table[c], index, axis=1, mode="promise_in_bounds")
                + part * jnp.take_along_axis(rise[c], index, axis=1, mode="promise_in_bounds")
                for c in range(4)
            ]
            facing = grad_x * light_x + grad_y * light_y + grad_z * light_z
            diffuse = (
                facing
                * facing
                / (grad_x * grad_x + grad_y * grad_y + grad_z * grad_z + SHADE_FLOOR)
            )
            shade = 0.25 + 0.75 * diffuse
            alpha = 1.0 - jnp.exp(scale * looked[3] * jax.nn.sigmoid(mixture))
            covered = through * alpha
            shaded = covered * shade
            for c in range(3):
                total[c] = total[c] + shaded * looked[c]
            through = through - covered
        at = pl.multiple_of(r * 32, 32)
        for c in range(3):
            out[pl.ds(at + c * 8, 8), :] = total[c]
        out[pl.ds(at + 24, 8), :] = 1.0 - through
        return carry

    lax.fori_loop(0, 8, tile, 0)


def over_kernel(pieces, out):
    total = [pieces[pl.ds(c * 8, 8), :] for c in range(4)]
    for k in range(1, 8):
        through = 1.0 - total[3]
        for c in range(4):
            total[c] = total[c] + through * pieces[pl.ds(k * 32 + c * 8, 8), :]
    for c in range(4):
        out[pl.ds(c * 8, 8), :] = total[c]


def vmem():
    return pl.BlockSpec(memory_space=pltpu.VMEM)


def call(kernel, name, args, outs, scratch=(), smem=0):
    return pl.pallas_call(
        kernel,
        name=name,
        out_shape=[jax.ShapeDtypeStruct(shape, F32) for shape in outs],
        in_specs=[pl.BlockSpec(memory_space=pltpu.SMEM)] * smem + [vmem()] * (len(args) - smem),
        out_specs=[vmem()] * len(outs),
        scratch_shapes=[pltpu.VMEM(shape, F32) for shape in scratch],
        compiler_params=pltpu.CompilerParams(vmem_limit_bytes=16 * 2**20),
    )(*args)


def swap(inner, outer, axis):
    size = lax.axis_size(axis)
    pairs = [[(i, i + 1), (i + 1, i)] for i in range(size - 1)]
    return (
        lax.ppermute(inner, axis, sum(pairs[0::2], [])),
        lax.ppermute(outer, axis, sum(pairs[1::2], [])),
    )


def even(axis):
    return lax.axis_index(axis) % 2 == 0


def shards(field, transfer, light_angles):
    depth_count = lax.axis_size("gz")
    depth_step = 1.0 / (field.shape[1] * depth_count)
    field = field.reshape(2048, 128)
    inner, outer = swap(
        *call(faces_kernel, "faces", (field,), ((384, 128), (384, 128))), "gz"
    )
    depth, to_inner, to_outer = call(
        depth_kernel, "depth", (field, inner, outer), ((3072, 128), (144, 128), (144, 128))
    )
    inner, outer = swap(to_inner, to_outer, "gx")
    cross, to_inner, to_outer = call(
        cross_kernel,
        "cross",
        (depth, inner, outer),
        ((4096, 128), (128, 128), (128, 128)),
        ((2304, 128),),
    )
    inner, outer = swap(to_inner, to_outer, "gy")
    rows, light = call(
        row_kernel, "rows", (light_angles, cross, jnp.asarray(row_matrix())), ((5120, 128), (24, 128)), (), 1
    )
    (partial_value,) = call(
        functools.partial(sample_kernel, scale=-OPTICAL * depth_step),
        "sample",
        (light, rows, inner, outer, jnp.asarray(edge_matrix()), transfer),
        ((256, 128),),
        ((5120, 128),),
    )
    pieces = lax.all_to_all(partial_value.reshape(8, 32, 128), "gz", 0, 0)
    (image,) = call(over_kernel, "over", (pieces.reshape(256, 128),), ((32, 128),))
    return image.reshape(4, 8, 128)


def solution(mesh):
    placed = (P(None, "gz", "gx", "gy"), P(), P())
    return jax.shard_map(
        shards, mesh=mesh, in_specs=placed, out_specs=P(None, ("gx", "gz"), "gy"), check_vma=False
    )
```

```python
import functools
import math

import jax
import jax.numpy as jnp
import numpy as np
from jax import lax
from jax.experimental import pallas as pl
from jax.experimental.pallas import tpu as pltpu
from jax.sharding import PartitionSpec as P

SIGMA_TAPS = 1.2
OPTICAL = 2.0
SHADE_FLOOR = 0.25
F32 = jnp.float32
BF16 = jnp.bfloat16


def filter_taps():
    places = [-3, -2, -1, 0, 1, 2, 3]
    bell = [math.exp(-place * place / (2.0 * SIGMA_TAPS * SIGMA_TAPS)) for place in places]
    bell_total = sum(bell)
    slope_total = sum((place * place * weight for place, weight in zip(places, bell)))
    smooth_taps = [weight / bell_total for weight in bell]
    slope_taps = [place * weight / slope_total for place, weight in zip(places, bell)]
    return (smooth_taps, slope_taps)


SMOOTH, SLOPE = filter_taps()


def smooth7(v):
    return (
        SMOOTH[3] * v[3]
        + SMOOTH[4] * (v[2] + v[4])
        + SMOOTH[5] * (v[1] + v[5])
        + SMOOTH[6] * (v[0] + v[6])
    )


def slope7(v):
    return SLOPE[4] * (v[4] - v[2]) + SLOPE[5] * (v[5] - v[1]) + SLOPE[6] * (v[6] - v[0])


INSIDE = list(range(3, 13))
BORDER = [0, 1, 2, 13, 14, 15]


def place_of(d):
    return (True, d - 3) if 3 <= d <= 12 else (False, BORDER.index(d))


def faces_kernel(field, to_inner, to_outer):
    even_z = even("gz")
    for f in range(2):
        for k in range(0, 192, 64):
            low = field[pl.ds(f * 1024 + k, 64), :]
            high = field[pl.ds(f * 1024 + 832 + k, 64), :]
            to_inner[pl.ds(f * 192 + k, 64), :] = jnp.where(even_z, high, low)
            to_outer[pl.ds(f * 192 + k, 64), :] = jnp.where(even_z, low, high)


def inside_kernel(angles, field, out, light):
    azimuth = jnp.full((8, 128), angles[0])
    polar = jnp.full((8, 128), angles[1])
    light[0:8, :] = jnp.cos(azimuth) * jnp.sin(polar)
    light[8:16, :] = jnp.sin(azimuth) * jnp.sin(polar)
    light[16:24, :] = jnp.cos(polar)

    def tile(r, carry):
        at = pl.multiple_of(r * 8, 8)
        first = [field[pl.ds(d * 64 + at, 8), :] for d in range(16)]
        second = [field[pl.ds(1024 + d * 64 + at, 8), :] for d in range(16)]
        for k in range(10):
            out[pl.ds(k * 64 + at, 8), :] = smooth7(first[k : k + 7])
            out[pl.ds(640 + k * 64 + at, 8), :] = slope7(first[k : k + 7])
            out[pl.ds(1280 + k * 64 + at, 8), :] = smooth7(second[k : k + 7])
        return carry

    lax.fori_loop(0, 8, tile, 0)


def border_kernel(field, inside, inner, outer, out, to_inner, to_outer):
    even_z = even("gz")
    even_x = even("gx")

    def tile(r, carry):
        at = pl.multiple_of(r * 8, 8)

        def plane(f, d):
            if d < 0:
                rows = pl.ds(f * 192 + (d + 3) * 64 + at, 8)
                return jnp.where(even_z, outer[rows, :], inner[rows, :])
            if d > 15:
                rows = pl.ds(f * 192 + (d - 16) * 64 + at, 8)
                return jnp.where(even_z, inner[rows, :], outer[rows, :])
            return field[pl.ds(f * 1024 + d * 64 + at, 8), :]

        for half in range(2):
            start = 13 * half
            first = [plane(0, d) for d in range(start - 3, start + 6)]
            second = [plane(1, d) for d in range(start - 3, start + 6)]
            for k in range(3):
                row = (half * 3 + k) * 64 + at
                out[pl.ds(row, 8), :] = smooth7(first[k : k + 7])
                out[pl.ds(384 + row, 8), :] = slope7(first[k : k + 7])
                out[pl.ds(768 + row, 8), :] = smooth7(second[k : k + 7])
        return carry

    lax.fori_loop(0, 8, tile, 0)
    for j in range(3):
        for f in range(3):
            at = j * 48 + f * 16
            for source, planes, first in ((inside, 10, at), (out, 6, at + 10)):
                base = f * planes * 64 + j
                low = source[pl.ds(base, planes, stride=64), :]
                high = source[pl.ds(base + 61, planes, stride=64), :]
                to_inner[pl.ds(first, planes), :] = jnp.where(even_x, high, low)
                to_outer[pl.ds(first, planes), :] = jnp.where(even_x, low, high)


def source_rows(inside, border, f, d):
    inner, k = place_of(d)
    return (inside, (f * 10 + k) * 64) if inner else (border, (f * 6 + k) * 64)


def collect(slot, packed, d, value):
    return jnp.where(slot == d, pltpu.roll(value, (8 * d + 3) % 128, 1), packed)


def filtered_columns(f, v):
    return [(0, smooth7(v)), (1, slope7(v))] if f == 0 else [(f + 1, smooth7(v))]


def middle_kernel(inside, border, out, edges):
    slot = lax.broadcasted_iota(jnp.int32, (8, 128), 1) // 8
    for f in range(3):
        packed = {}
        for d in range(16):
            source, base = source_rows(inside, border, f, d)
            for r in range(1, 7):
                first = base + r * 8 - 3
                v = [source[first + k : first + k + 8, :] for k in range(7)]
                for g, value in filtered_columns(f, v):
                    row = g * 768 + d * 48 + (r - 1) * 8
                    out[row : row + 8, :] = value
                    packed[g, r] = collect(slot, packed.get((g, r), 0.0), d, value)
        for (g, r), value in packed.items():
            edges[g * 48 + (r - 1) * 8 : g * 48 + r * 8, :] = value


def ends_kernel(inside, border, edges, inner, outer, out, to_inner, to_outer, edge):
    even_x = even("gx")
    even_y = even("gy")
    lane = lax.broadcasted_iota(jnp.int32, (8, 128), 1)
    slot = lane // 8
    firsthalf = lane % 8 < 3
    for f in range(3):
        packed = {}
        for d in range(16):
            source, base = source_rows(inside, border, f, d)
            whole, k = place_of(d)
            at = f * 16 + (k if whole else 10 + k)
            e = (f * 16 + d) * 48
            a = inner[pl.ds(at, 3, stride=48), :]
            b = outer[pl.ds(at, 3, stride=48), :]
            edge[e + 5 : e + 8, :] = jnp.where(even_x, b, a)
            edge[e + 8 : e + 24, :] = source[base : base + 16, :]
            edge[e + 24 : e + 40, :] = source[base + 48 : base + 64, :]
            edge[e + 40 : e + 43, :] = jnp.where(even_x, a, b)
            for r, first in ((0, e + 5), (7, e + 29)):
                v = [edge[first + k : first + k + 8, :] for k in range(7)]
                for g, value in filtered_columns(f, v):
                    row = g * 256 + d * 16 + (8 if r else 0)
                    out[row : row + 8, :] = value
                    packed[g, r] = collect(slot, packed.get((g, r), 0.0), d, value)
        for g in sorted({g for g, r in packed}):
            tiles = [packed[g, 0]]
            tiles += [edges[g * 48 + r * 8 : g * 48 + r * 8 + 8, :] for r in range(6)]
            tiles += [packed[g, 7]]
            for q in range(4):
                a, b = tiles[2 * q : 2 * q + 2]
                at = g * 32 + q * 8
                up = jnp.where(firsthalf, a, pltpu.roll(b, 3, 1))
                down = jnp.where(firsthalf, pltpu.roll(a, 125, 1), b)
                to_inner[at : at + 8, :] = jnp.where(even_y, up, down)
                to_outer[at : at + 8, :] = jnp.where(even_y, down, up)


def lanes_from(value, offset):
    return pltpu.roll(value, -offset % 128, 1)


def row_matrix():
    matrix = np.zeros((128, 256), np.float64)
    for j in range(128):
        for o in range(-3, 4):
            if 0 <= j + o < 128:
                matrix[j + o, j] = SMOOTH[o + 3]
                matrix[j + o, 128 + j] = SLOPE[o + 3]
    matrix = matrix.astype(np.float32)
    high = matrix.astype(jnp.bfloat16)
    low = (matrix - high.astype(np.float32)).astype(jnp.bfloat16)
    return np.concatenate([high, high, low, low], axis=0)


def row_kernel(middle, ends, matrix, out):
    def filtered(g, weights):
        rows = jnp.concatenate(
            [
                middle[pl.ds(pl.multiple_of(g * 768, 768), 768), :],
                ends[pl.ds(pl.multiple_of(g * 256, 256), 256), :],
            ],
            axis=0,
        )
        high = rows.astype(BF16)
        low = (rows - high.astype(F32)).astype(BF16)
        cells = jnp.concatenate([high, low, high, low], axis=1)
        return jnp.dot(cells, weights, preferred_element_type=F32)

    both = filtered(0, matrix[...])
    out[0:1024, :] = both[:, 0:128]
    out[4096:5120, :] = both[:, 128:256]

    def rest(g, carry):
        at = pl.ds(pl.multiple_of(g * 1024, 1024), 1024)
        out[at, :] = filtered(g, matrix[:, 0:128])
        return carry

    lax.fori_loop(1, 4, rest, 0)


def edge_matrix():
    matrix = np.zeros((256, 512), np.float32)
    for d in range(16):
        for h in range(2):
            for lane in range(6):
                for o in (-3, -2, -1, 1, 2, 3):
                    cell = lane + o
                    if 0 <= cell < 6 and (lane < 3) == (o > 0) and (lane < 3) != (cell < 3):
                        row = 8 * d + 3 * h + cell % 3 + (128 if cell >= 3 else 0)
                        column = 256 * h + 8 * d + lane
                        matrix[row, column] = SMOOTH[o + 3]
                        matrix[row, column + 128] = SLOPE[o + 3]
    return matrix


def place_matrix():
    matrix = np.zeros((256, 2048), np.float32)
    for d in range(16):
        for lane in range(6):
            matrix[8 * d + lane, d * 128 + (lane + 125) % 128] = 1.0
            matrix[128 + 8 * d + lane, d * 128 + (lane + 125) % 128] = 1.0
    return matrix.astype(jnp.bfloat16)


def sample_kernel(
    light, source, inner, outer, matrix, places, transfer, out, grids, *, scale
):
    even_y = even("gy")
    lane = lax.broadcasted_iota(jnp.int32, (8, 128), 1)
    left = jnp.where(even_y, outer[...], inner[...])
    right = jnp.where(even_y, inner[...], outer[...])
    terms = jnp.dot(
        jnp.concatenate([left, right], axis=1),
        matrix[...],
        precision=lax.Precision.HIGHEST,
        preferred_element_type=F32,
    )
    packed = jnp.concatenate(
        [
            terms[(g % 4) * 32 + (r // 2) * 8 :][:8, (r % 2) * 256 + (128 if g == 4 else 0) :][:, :128]
            for g in range(5)
            for r in range(8)
        ],
        axis=0,
    )
    high = packed.astype(BF16)
    low = (packed - high.astype(F32)).astype(BF16)
    packed = jnp.concatenate([high, low], axis=1)
    for pair in range(8):
        moved = jnp.dot(
            packed, places[:, pair * 256 : pair * 256 + 256], preferred_element_type=F32
        )
        for g in range(5):
            for r in range(8):
                for h in range(2):
                    d = pair * 2 + h
                    at = g * 1024 + d * 64 + r * 8
                    inside = 0 < r < 7
                    row = g * 1024 + (d * 48 + r * 8 - 8 if inside else 768 + d * 16 + r // 7 * 8)
                    grids[at : at + 8, :] = (
                        source[row : row + 8, :]
                        + moved[g * 64 + r * 8 : g * 64 + r * 8 + 8, h * 128 : h * 128 + 128]
                    )

    bins = 128
    step = 3.0 / 32760.0
    table = []
    for c in range(4):
        entry = jnp.round(jnp.broadcast_to(transfer[c : c + 1, :], (8, bins)) * (1.0 / step))
        rise = jnp.where(lane < bins - 1, lanes_from(entry, 1) - entry, 0.0)
        table.append(entry.astype(jnp.int32) * 65536 + (rise.astype(jnp.int32) & 65535))
    light_x, light_y, light_z = light[0:8, :], light[8:16, :], light[16:24, :]
    def tile(r, carry):
        total = [jnp.zeros((8, 128), F32)] * 3
        through = jnp.ones((8, 128), F32)
        for d in range(16):
            at = pl.multiple_of(d * 64 + r * 8, 8)
            value, grad_x, grad_z, mixture, grad_y = [
                grids[pl.ds(g * 1024 + at, 8), :] for g in range(5)
            ]
            position = jax.nn.sigmoid(value) * (bins - 1)
            whole = jnp.floor(position)
            part = position - whole
            index = whole.astype(jnp.int32)
            looked = []
            for c in range(4):
                both = jnp.take_along_axis(table[c], index, axis=1, mode="promise_in_bounds")
                entry = lax.shift_right_arithmetic(both, 16).astype(F32)
                rise = lax.shift_right_arithmetic(lax.shift_left(both, 16), 16).astype(F32)
                looked.append(entry + part * rise)
            facing = grad_x * light_x + grad_y * light_y + grad_z * light_z
            diffuse = (
                facing
                * facing
                / (grad_x * grad_x + grad_y * grad_y + grad_z * grad_z + SHADE_FLOOR)
            )
            shade = 0.25 + 0.75 * diffuse
            alpha = 1.0 - jnp.exp(scale * step * looked[3] * jax.nn.sigmoid(mixture))
            covered = through * alpha
            shaded = covered * shade
            for c in range(3):
                total[c] = total[c] + shaded * looked[c]
            through = through - covered
        at = pl.multiple_of(r * 32, 32)
        for c in range(3):
            out[pl.ds(at + c * 8, 8), :] = total[c] * step
        out[pl.ds(at + 24, 8), :] = 1.0 - through
        return carry

    lax.fori_loop(0, 8, tile, 0)


def over_kernel(pieces, out):
    total = [pieces[pl.ds(c * 8, 8), :] for c in range(4)]
    for k in range(1, 8):
        through = 1.0 - total[3]
        for c in range(4):
            total[c] = total[c] + through * pieces[pl.ds(k * 32 + c * 8, 8), :]
    for c in range(4):
        out[pl.ds(c * 8, 8), :] = total[c]


VMEM = pl.BlockSpec(memory_space=pltpu.VMEM)
SMEM = pl.BlockSpec(memory_space=pltpu.SMEM)


def call(kernel, name, args, outs, scratch=(), spaces=None):
    return pl.pallas_call(
        kernel,
        name=name,
        out_shape=[jax.ShapeDtypeStruct(shape, F32) for shape in outs],
        in_specs=spaces or [VMEM] * len(args),
        out_specs=[VMEM] * len(outs),
        scratch_shapes=scratch,
        compiler_params=pltpu.CompilerParams(vmem_limit_bytes=16 * 2**20),
    )(*args)


def swap(inner, outer, axis):
    size = lax.axis_size(axis)
    pairs = [[(i, i + 1), (i + 1, i)] for i in range(size - 1)]
    return (
        lax.ppermute(inner, axis, sum(pairs[0::2], [])),
        lax.ppermute(outer, axis, sum(pairs[1::2], [])),
    )


def even(axis):
    return lax.axis_index(axis) % 2 == 0


def shards(field, transfer, light_angles):
    depth_count = lax.axis_size("gz")
    depth_step = 1.0 / (field.shape[1] * depth_count)
    field = field.reshape(2048, 128)
    faces = call(faces_kernel, "faces", (field,), ((384, 128), (384, 128)))
    inner, outer = swap(*faces, "gz")
    inside, light = call(
        inside_kernel, "inside", (light_angles, field), ((1920, 128), (24, 128)), (), [SMEM, VMEM]
    )
    border, to_inner, to_outer = call(
        border_kernel,
        "border",
        (field, inside, inner, outer),
        ((1152, 128), (144, 128), (144, 128)),
    )
    inner, outer = swap(to_inner, to_outer, "gx")
    middle, edges = call(middle_kernel, "middle", (inside, border), ((3072, 128), (192, 128)))
    ends, to_inner, to_outer = call(
        ends_kernel,
        "ends",
        (inside, border, edges, inner, outer),
        ((1024, 128), (128, 128), (128, 128)),
        [pltpu.VMEM((2304, 128), F32)],
    )
    inner, outer = swap(to_inner, to_outer, "gy")
    (rows,) = call(row_kernel, "rows", (middle, ends, jnp.asarray(row_matrix())), ((5120, 128),))
    (partial_value,) = call(
        functools.partial(sample_kernel, scale=-OPTICAL * depth_step),
        "sample",
        (
            light,
            rows,
            inner,
            outer,
            jnp.asarray(edge_matrix()),
            jnp.asarray(place_matrix()),
            transfer,
        ),
        ((256, 128),),
        [pltpu.VMEM((5120, 128), F32)],
    )
    pieces = lax.all_to_all(partial_value.reshape(8, 32, 128), "gz", 0, 0)
    (image,) = call(over_kernel, "over", (pieces.reshape(256, 128),), ((32, 128),))
    return image.reshape(4, 8, 128)


def solution(mesh):
    placed = (P(None, "gz", "gx", "gy"), P(), P())
    return jax.shard_map(
        shards, mesh=mesh, in_specs=placed, out_specs=P(None, ("gx", "gz"), "gy"), check_vma=False
    )
```

```python
import functools
import math

import jax
import jax.numpy as jnp
import numpy as np
from jax import lax
from jax.experimental import pallas as pl
from jax.experimental.pallas import tpu as pltpu
from jax.sharding import PartitionSpec as P

SIGMA_TAPS = 1.2
OPTICAL = 2.0
SHADE_FLOOR = 0.25
F32 = jnp.float32
BF16 = jnp.bfloat16


def filter_taps():
    places = [-3, -2, -1, 0, 1, 2, 3]
    bell = [math.exp(-place * place / (2.0 * SIGMA_TAPS * SIGMA_TAPS)) for place in places]
    bell_total = sum(bell)
    slope_total = sum((place * place * weight for place, weight in zip(places, bell)))
    smooth_taps = [weight / bell_total for weight in bell]
    slope_taps = [place * weight / slope_total for place, weight in zip(places, bell)]
    return (smooth_taps, slope_taps)


SMOOTH, SLOPE = filter_taps()


def smooth7(v):
    return (
        SMOOTH[3] * v[3]
        + SMOOTH[4] * (v[2] + v[4])
        + SMOOTH[5] * (v[1] + v[5])
        + SMOOTH[6] * (v[0] + v[6])
    )


def slope7(v):
    return SLOPE[4] * (v[4] - v[2]) + SLOPE[5] * (v[5] - v[1]) + SLOPE[6] * (v[6] - v[0])


INSIDE = list(range(3, 13))
BORDER = [0, 1, 2, 13, 14, 15]


def place_of(d):
    return (True, d - 3) if 3 <= d <= 12 else (False, BORDER.index(d))


def faces_kernel(field, to_inner, to_outer):
    even_z = even("gz")
    for f in range(2):
        for k in range(0, 192, 64):
            low = field[pl.ds(f * 1024 + k, 64), :]
            high = field[pl.ds(f * 1024 + 832 + k, 64), :]
            to_inner[pl.ds(f * 192 + k, 64), :] = jnp.where(even_z, high, low)
            to_outer[pl.ds(f * 192 + k, 64), :] = jnp.where(even_z, low, high)


def inside_kernel(angles, field, out, light):
    azimuth = jnp.full((8, 128), angles[0])
    polar = jnp.full((8, 128), angles[1])
    light[0:8, :] = jnp.cos(azimuth) * jnp.sin(polar)
    light[8:16, :] = jnp.sin(azimuth) * jnp.sin(polar)
    light[16:24, :] = jnp.cos(polar)

    def tile(r, carry):
        at = pl.multiple_of(r * 8, 8)
        first = [field[pl.ds(d * 64 + at, 8), :] for d in range(16)]
        second = [field[pl.ds(1024 + d * 64 + at, 8), :] for d in range(16)]
        for k in range(10):
            out[pl.ds(k * 64 + at, 8), :] = smooth7(first[k : k + 7])
            out[pl.ds(640 + k * 64 + at, 8), :] = slope7(first[k : k + 7])
            out[pl.ds(1280 + k * 64 + at, 8), :] = smooth7(second[k : k + 7])
        return carry

    lax.fori_loop(0, 8, tile, 0)


def border_rows(field, inner, outer, out, at, to):
    even_z = even("gz")

    def plane(f, d):
        if d < 0:
            rows = pl.ds(f * 192 + (d + 3) * 64 + at, 8)
            return jnp.where(even_z, outer[rows, :], inner[rows, :])
        if d > 15:
            rows = pl.ds(f * 192 + (d - 16) * 64 + at, 8)
            return jnp.where(even_z, inner[rows, :], outer[rows, :])
        return field[pl.ds(f * 1024 + d * 64 + at, 8), :]

    stride = out.shape[0] // 18
    for half in range(2):
        start = 13 * half
        first = [plane(0, d) for d in range(start - 3, start + 6)]
        second = [plane(1, d) for d in range(start - 3, start + 6)]
        for k in range(3):
            row = (half * 3 + k) * stride + to
            out[pl.ds(row, 8), :] = smooth7(first[k : k + 7])
            out[pl.ds(6 * stride + row, 8), :] = slope7(first[k : k + 7])
            out[pl.ds(12 * stride + row, 8), :] = smooth7(second[k : k + 7])


def cross_faces_kernel(field, inside, inner, outer, to_inner, to_outer, ends):
    even_x = even("gx")
    border_rows(field, inner, outer, ends, 0, 0)
    border_rows(field, inner, outer, ends, 56, 8)
    for j in range(3):
        for f in range(3):
            at = j * 48 + f * 16
            for source, planes, first, size in ((inside, 10, at, 64), (ends, 6, at + 10, 16)):
                base = f * planes * size + j
                low = source[pl.ds(base, planes, stride=size), :]
                high = source[pl.ds(base + size - 3, planes, stride=size), :]
                to_inner[pl.ds(first, planes), :] = jnp.where(even_x, high, low)
                to_outer[pl.ds(first, planes), :] = jnp.where(even_x, low, high)


def border_kernel(field, inner, outer, out):
    def tile(r, carry):
        at = pl.multiple_of(r * 8, 8)
        border_rows(field, inner, outer, out, at, at)
        return carry

    lax.fori_loop(0, 8, tile, 0)


def source_rows(inside, border, f, d):
    inner, k = place_of(d)
    return (inside, (f * 10 + k) * 64) if inner else (border, (f * 6 + k) * 64)


def collect(slot, packed, d, value):
    return jnp.where(slot == d, pltpu.roll(value, (8 * d + 3) % 128, 1), packed)


def filtered_columns(f, v):
    return [(0, smooth7(v)), (1, slope7(v))] if f == 0 else [(f + 1, smooth7(v))]


def middle_kernel(inside, border, out, edges):
    slot = lax.broadcasted_iota(jnp.int32, (8, 128), 1) // 8
    for f in range(3):
        packed = {}
        for d in range(16):
            source, base = source_rows(inside, border, f, d)
            for r in range(1, 7):
                first = base + r * 8 - 3
                v = [source[first + k : first + k + 8, :] for k in range(7)]
                for g, value in filtered_columns(f, v):
                    row = g * 768 + d * 48 + (r - 1) * 8
                    out[row : row + 8, :] = value
                    packed[g, r] = collect(slot, packed.get((g, r), 0.0), d, value)
        for (g, r), value in packed.items():
            edges[g * 48 + (r - 1) * 8 : g * 48 + r * 8, :] = value


def ends_kernel(inside, border, edges, inner, outer, out, to_inner, to_outer, edge):
    even_x = even("gx")
    even_y = even("gy")
    lane = lax.broadcasted_iota(jnp.int32, (8, 128), 1)
    slot = lane // 8
    firsthalf = lane % 8 < 3
    for f in range(3):
        packed = {}
        for d in range(16):
            source, base = source_rows(inside, border, f, d)
            whole, k = place_of(d)
            at = f * 16 + (k if whole else 10 + k)
            e = (f * 16 + d) * 48
            a = inner[pl.ds(at, 3, stride=48), :]
            b = outer[pl.ds(at, 3, stride=48), :]
            edge[e + 5 : e + 8, :] = jnp.where(even_x, b, a)
            edge[e + 8 : e + 24, :] = source[base : base + 16, :]
            edge[e + 24 : e + 40, :] = source[base + 48 : base + 64, :]
            edge[e + 40 : e + 43, :] = jnp.where(even_x, a, b)
            for r, first in ((0, e + 5), (7, e + 29)):
                v = [edge[first + k : first + k + 8, :] for k in range(7)]
                for g, value in filtered_columns(f, v):
                    row = g * 256 + d * 16 + (8 if r else 0)
                    out[row : row + 8, :] = value
                    packed[g, r] = collect(slot, packed.get((g, r), 0.0), d, value)
        for g in sorted({g for g, r in packed}):
            tiles = [packed[g, 0]]
            tiles += [edges[g * 48 + r * 8 : g * 48 + r * 8 + 8, :] for r in range(6)]
            tiles += [packed[g, 7]]
            for q in range(4):
                a, b = tiles[2 * q : 2 * q + 2]
                at = g * 32 + q * 8
                up = jnp.where(firsthalf, a, pltpu.roll(b, 3, 1))
                down = jnp.where(firsthalf, pltpu.roll(a, 125, 1), b)
                to_inner[at : at + 8, :] = jnp.where(even_y, up, down)
                to_outer[at : at + 8, :] = jnp.where(even_y, down, up)


def lanes_from(value, offset):
    return pltpu.roll(value, -offset % 128, 1)


def row_matrix():
    matrix = np.zeros((128, 256), np.float64)
    for j in range(128):
        for o in range(-3, 4):
            if 0 <= j + o < 128:
                matrix[j + o, j] = SMOOTH[o + 3]
                matrix[j + o, 128 + j] = SLOPE[o + 3]
    matrix = matrix.astype(np.float32)
    high = matrix.astype(jnp.bfloat16)
    low = (matrix - high.astype(np.float32)).astype(jnp.bfloat16)
    return np.concatenate([high, high, low, low], axis=0)


def row_kernel(middle, ends, matrix, out):
    def filtered(g, weights):
        rows = jnp.concatenate(
            [
                middle[pl.ds(pl.multiple_of(g * 768, 768), 768), :],
                ends[pl.ds(pl.multiple_of(g * 256, 256), 256), :],
            ],
            axis=0,
        )
        high = rows.astype(BF16)
        low = (rows - high.astype(F32)).astype(BF16)
        cells = jnp.concatenate([high, low, high, low], axis=1)
        return jnp.dot(cells, weights, preferred_element_type=F32)

    both = filtered(0, matrix[...])
    out[0:1024, :] = both[:, 0:128]
    out[4096:5120, :] = both[:, 128:256]

    def rest(g, carry):
        at = pl.ds(pl.multiple_of(g * 1024, 1024), 1024)
        out[at, :] = filtered(g, matrix[:, 0:128])
        return carry

    lax.fori_loop(1, 4, rest, 0)


def edge_matrix():
    matrix = np.zeros((256, 512), np.float32)
    for d in range(16):
        for h in range(2):
            for lane in range(6):
                for o in (-3, -2, -1, 1, 2, 3):
                    cell = lane + o
                    if 0 <= cell < 6 and (lane < 3) == (o > 0) and (lane < 3) != (cell < 3):
                        row = 8 * d + 3 * h + cell % 3 + (128 if cell >= 3 else 0)
                        column = 256 * h + 8 * d + lane
                        matrix[row, column] = SMOOTH[o + 3]
                        matrix[row, column + 128] = SLOPE[o + 3]
    return matrix


def place_matrix():
    matrix = np.zeros((256, 2048), np.float32)
    for d in range(16):
        for lane in range(6):
            matrix[8 * d + lane, d * 128 + (lane + 125) % 128] = 1.0
            matrix[128 + 8 * d + lane, d * 128 + (lane + 125) % 128] = 1.0
    return matrix.astype(jnp.bfloat16)


def sample_kernel(
    light, source, inner, outer, matrix, places, transfer, out, grids, *, scale
):
    even_y = even("gy")
    lane = lax.broadcasted_iota(jnp.int32, (8, 128), 1)
    left = jnp.where(even_y, outer[...], inner[...])
    right = jnp.where(even_y, inner[...], outer[...])
    terms = jnp.dot(
        jnp.concatenate([left, right], axis=1),
        matrix[...],
        precision=lax.Precision.HIGHEST,
        preferred_element_type=F32,
    )
    packed = jnp.concatenate(
        [
            terms[(g % 4) * 32 + (r // 2) * 8 :][:8, (r % 2) * 256 + (128 if g == 4 else 0) :][:, :128]
            for g in range(5)
            for r in range(8)
        ],
        axis=0,
    )
    high = packed.astype(BF16)
    low = (packed - high.astype(F32)).astype(BF16)
    packed = jnp.concatenate([high, low], axis=1)
    for pair in range(8):
        moved = jnp.dot(
            packed, places[:, pair * 256 : pair * 256 + 256], preferred_element_type=F32
        )
        for g in range(5):
            for r in range(8):
                for h in range(2):
                    d = pair * 2 + h
                    at = g * 1024 + d * 64 + r * 8
                    inside = 0 < r < 7
                    row = g * 1024 + (d * 48 + r * 8 - 8 if inside else 768 + d * 16 + r // 7 * 8)
                    grids[at : at + 8, :] = (
                        source[row : row + 8, :]
                        + moved[g * 64 + r * 8 : g * 64 + r * 8 + 8, h * 128 : h * 128 + 128]
                    )

    bins = 128
    step = 3.0 / 32760.0
    table = []
    for c in range(4):
        entry = jnp.round(jnp.broadcast_to(transfer[c : c + 1, :], (8, bins)) * (1.0 / step))
        rise = jnp.where(lane < bins - 1, lanes_from(entry, 1) - entry, 0.0)
        table.append(entry.astype(jnp.int32) * 65536 + (rise.astype(jnp.int32) & 65535))
    light_x, light_y, light_z = light[0:8, :], light[8:16, :], light[16:24, :]
    def tile(r, carry):
        total = [jnp.zeros((8, 128), F32)] * 3
        through = jnp.ones((8, 128), F32)
        for d in range(16):
            at = pl.multiple_of(d * 64 + r * 8, 8)
            value, grad_x, grad_z, mixture, grad_y = [
                grids[pl.ds(g * 1024 + at, 8), :] for g in range(5)
            ]
            position = jax.nn.sigmoid(value) * (bins - 1)
            whole = jnp.floor(position)
            part = position - whole
            index = whole.astype(jnp.int32)
            looked = []
            for c in range(4):
                both = jnp.take_along_axis(table[c], index, axis=1, mode="promise_in_bounds")
                entry = lax.shift_right_arithmetic(both, 16).astype(F32)
                rise = lax.shift_right_arithmetic(lax.shift_left(both, 16), 16).astype(F32)
                looked.append(entry + part * rise)
            facing = grad_x * light_x + grad_y * light_y + grad_z * light_z
            diffuse = (
                facing
                * facing
                / (grad_x * grad_x + grad_y * grad_y + grad_z * grad_z + SHADE_FLOOR)
            )
            shade = 0.25 + 0.75 * diffuse
            alpha = 1.0 - jnp.exp(scale * step * looked[3] * jax.nn.sigmoid(mixture))
            covered = through * alpha
            shaded = covered * shade
            for c in range(3):
                total[c] = total[c] + shaded * looked[c]
            through = through - covered
        at = pl.multiple_of(r * 32, 32)
        for c in range(3):
            out[pl.ds(at + c * 8, 8), :] = total[c] * step
        out[pl.ds(at + 24, 8), :] = 1.0 - through
        return carry

    lax.fori_loop(0, 8, tile, 0)


def over_kernel(pieces, out):
    total = [pieces[pl.ds(c * 8, 8), :] for c in range(4)]
    for k in range(1, 8):
        through = 1.0 - total[3]
        for c in range(4):
            total[c] = total[c] + through * pieces[pl.ds(k * 32 + c * 8, 8), :]
    for c in range(4):
        out[pl.ds(c * 8, 8), :] = total[c]


VMEM = pl.BlockSpec(memory_space=pltpu.VMEM)
SMEM = pl.BlockSpec(memory_space=pltpu.SMEM)


def call(kernel, name, args, outs, scratch=(), spaces=None):
    return pl.pallas_call(
        kernel,
        name=name,
        out_shape=[jax.ShapeDtypeStruct(shape, F32) for shape in outs],
        in_specs=spaces or [VMEM] * len(args),
        out_specs=[VMEM] * len(outs),
        scratch_shapes=scratch,
        compiler_params=pltpu.CompilerParams(vmem_limit_bytes=16 * 2**20),
    )(*args)


def swap(inner, outer, axis):
    size = lax.axis_size(axis)
    lines = 1 if axis == "gy" else lax.axis_size("gy")
    exchanges = ([], [])
    for line in range(lines):
        for i in range(size):
            for turn in range(2):
                other = i + 1 if (i + line + turn) % 2 == 0 else i - 1
                if 0 <= other < size:
                    pair = (i, other)
                    if axis == "gz":
                        pair = (line * size + i, line * size + other)
                    if axis == "gx":
                        pair = (i * lines + line, other * lines + line)
                    exchanges[turn].append(pair)
    axes = {"gx": ("gx", "gy"), "gy": "gy", "gz": ("gy", "gz")}[axis]
    return lax.ppermute(inner, axes, exchanges[0]), lax.ppermute(outer, axes, exchanges[1])


def even(axis):
    line = 0 if axis == "gy" else lax.axis_index("gy")
    return (lax.axis_index(axis) + line) % 2 == 0


def shards(field, transfer, light_angles):
    depth_count = lax.axis_size("gz")
    depth_step = 1.0 / (field.shape[1] * depth_count)
    field = field.reshape(2048, 128)
    faces = call(faces_kernel, "faces", (field,), ((384, 128), (384, 128)))
    inner, outer = swap(*faces, "gz")
    inside, light = call(
        inside_kernel, "inside", (light_angles, field), ((1920, 128), (24, 128)), (), [SMEM, VMEM]
    )
    to_inner, to_outer = call(
        cross_faces_kernel,
        "cross_faces",
        (field, inside, inner, outer),
        ((144, 128), (144, 128)),
        [pltpu.VMEM((288, 128), F32)],
    )
    (border,) = call(border_kernel, "border", (field, inner, outer), ((1152, 128),))
    inner, outer = swap(to_inner, to_outer, "gx")
    middle, edges = call(middle_kernel, "middle", (inside, border), ((3072, 128), (192, 128)))
    ends, to_inner, to_outer = call(
        ends_kernel,
        "ends",
        (inside, border, edges, inner, outer),
        ((1024, 128), (128, 128), (128, 128)),
        [pltpu.VMEM((2304, 128), F32)],
    )
    inner, outer = swap(to_inner, to_outer, "gy")
    (rows,) = call(row_kernel, "rows", (middle, ends, jnp.asarray(row_matrix())), ((5120, 128),))
    (partial_value,) = call(
        functools.partial(sample_kernel, scale=-OPTICAL * depth_step),
        "sample",
        (
            light,
            rows,
            inner,
            outer,
            jnp.asarray(edge_matrix()),
            jnp.asarray(place_matrix()),
            transfer,
        ),
        ((256, 128),),
        [pltpu.VMEM((5120, 128), F32)],
    )
    pieces = lax.all_to_all(partial_value.reshape(8, 32, 128), "gz", 0, 0)
    (image,) = call(over_kernel, "over", (pieces.reshape(256, 128),), ((32, 128),))
    return image.reshape(4, 8, 128)


def solution(mesh):
    placed = (P(None, "gz", "gx", "gy"), P(), P())
    return jax.shard_map(
        shards, mesh=mesh, in_specs=placed, out_specs=P(None, ("gx", "gz"), "gy"), check_vma=False
    )
```

```python
import functools
import math

import jax
import jax.numpy as jnp
import numpy as np
from jax import lax
from jax.experimental import pallas as pl
from jax.experimental.pallas import tpu as pltpu
from jax.sharding import PartitionSpec as P

SIGMA_TAPS = 1.2
OPTICAL = 2.0
SHADE_FLOOR = 0.25
F32 = jnp.float32
BF16 = jnp.bfloat16


def filter_taps():
    places = [-3, -2, -1, 0, 1, 2, 3]
    bell = [math.exp(-place * place / (2.0 * SIGMA_TAPS * SIGMA_TAPS)) for place in places]
    bell_total = sum(bell)
    slope_total = sum((place * place * weight for place, weight in zip(places, bell)))
    smooth_taps = [weight / bell_total for weight in bell]
    slope_taps = [place * weight / slope_total for place, weight in zip(places, bell)]
    return (smooth_taps, slope_taps)


SMOOTH, SLOPE = filter_taps()


def smooth7(v):
    return (
        SMOOTH[3] * v[3]
        + SMOOTH[4] * (v[2] + v[4])
        + SMOOTH[5] * (v[1] + v[5])
        + SMOOTH[6] * (v[0] + v[6])
    )


def slope7(v):
    return SLOPE[4] * (v[4] - v[2]) + SLOPE[5] * (v[5] - v[1]) + SLOPE[6] * (v[6] - v[0])


INSIDE = list(range(3, 13))
BORDER = [0, 1, 2, 13, 14, 15]


def place_of(d):
    return (True, d - 3) if 3 <= d <= 12 else (False, BORDER.index(d))


def faces_kernel(field, to_inner, to_outer, done):
    high = pl.multiple_of(jnp.where(even("gz"), 832, 0), 64)
    copies = []
    for k, (target, first) in enumerate(((to_inner, high), (to_outer, 832 - high))):
        for f in range(2):
            rows = pl.ds(pl.multiple_of(f * 1024 + first, 64), 192)
            copies.append(
                pltpu.make_async_copy(
                    field.at[rows, :], target.at[pl.ds(f * 192, 192), :], done.at[2 * k + f]
                )
            )
    for copy in copies:
        copy.start()
    for copy in copies:
        copy.wait()


def inside_kernel(angles, field, out, light):
    azimuth = jnp.full((8, 128), angles[0])
    polar = jnp.full((8, 128), angles[1])
    light[0:8, :] = jnp.cos(azimuth) * jnp.sin(polar)
    light[8:16, :] = jnp.sin(azimuth) * jnp.sin(polar)
    light[16:24, :] = jnp.cos(polar)

    def tile(r, carry):
        at = pl.multiple_of(r * 8, 8)
        first = [field[pl.ds(d * 64 + at, 8), :] for d in range(16)]
        second = [field[pl.ds(1024 + d * 64 + at, 8), :] for d in range(16)]
        for k in range(10):
            out[pl.ds(k * 64 + at, 8), :] = smooth7(first[k : k + 7])
            out[pl.ds(640 + k * 64 + at, 8), :] = slope7(first[k : k + 7])
            out[pl.ds(1280 + k * 64 + at, 8), :] = smooth7(second[k : k + 7])
        return carry

    lax.fori_loop(0, 8, tile, 0)


def border_rows(field, inner, outer, out, at, to):
    even_z = even("gz")

    def plane(f, d):
        if d < 0:
            rows = pl.ds(f * 192 + (d + 3) * 64 + at, 8)
            return jnp.where(even_z, outer[rows, :], inner[rows, :])
        if d > 15:
            rows = pl.ds(f * 192 + (d - 16) * 64 + at, 8)
            return jnp.where(even_z, inner[rows, :], outer[rows, :])
        return field[pl.ds(f * 1024 + d * 64 + at, 8), :]

    stride = out.shape[0] // 18
    for half in range(2):
        start = 13 * half
        first = [plane(0, d) for d in range(start - 3, start + 6)]
        second = [plane(1, d) for d in range(start - 3, start + 6)]
        for k in range(3):
            row = (half * 3 + k) * stride + to
            out[pl.ds(row, 8), :] = smooth7(first[k : k + 7])
            out[pl.ds(6 * stride + row, 8), :] = slope7(first[k : k + 7])
            out[pl.ds(12 * stride + row, 8), :] = smooth7(second[k : k + 7])


def cross_faces_kernel(field, inside, inner, outer, to_inner, to_outer, ends):
    even_x = even("gx")
    border_rows(field, inner, outer, ends, 0, 0)
    border_rows(field, inner, outer, ends, 56, 8)
    for j in range(3):
        for f in range(3):
            at = j * 48 + f * 16
            for source, planes, first, size in ((inside, 10, at, 64), (ends, 6, at + 10, 16)):
                base = f * planes * size + j
                low = source[pl.ds(base, planes, stride=size), :]
                high = source[pl.ds(base + size - 3, planes, stride=size), :]
                to_inner[pl.ds(first, planes), :] = jnp.where(even_x, high, low)
                to_outer[pl.ds(first, planes), :] = jnp.where(even_x, low, high)


def border_kernel(field, inner, outer, out):
    def tile(r, carry):
        at = pl.multiple_of(r * 8, 8)
        border_rows(field, inner, outer, out, at, at)
        return carry

    lax.fori_loop(0, 8, tile, 0)


def source_rows(inside, border, f, d):
    inner, k = place_of(d)
    return (inside, (f * 10 + k) * 64) if inner else (border, (f * 6 + k) * 64)


def collect(slot, packed, d, value):
    return jnp.where(slot == d, pltpu.roll(value, (8 * d + 3) % 128, 1), packed)


def filtered_columns(f, v):
    return [(0, smooth7(v)), (1, slope7(v))] if f == 0 else [(f + 1, smooth7(v))]


def middle_kernel(inside, border, out, edges):
    slot = lax.broadcasted_iota(jnp.int32, (8, 128), 1) // 8
    for f in range(3):
        packed = {}
        for d in range(16):
            source, base = source_rows(inside, border, f, d)
            for r in range(1, 7):
                first = base + r * 8 - 3
                v = [source[first + k : first + k + 8, :] for k in range(7)]
                for g, value in filtered_columns(f, v):
                    row = g * 768 + d * 48 + (r - 1) * 8
                    out[row : row + 8, :] = value
                    packed[g, r] = collect(slot, packed.get((g, r), 0.0), d, value)
        for (g, r), value in packed.items():
            edges[g * 48 + (r - 1) * 8 : g * 48 + r * 8, :] = value


def ends_kernel(inside, border, edges, inner, outer, out, to_inner, to_outer, edge):
    even_x = even("gx")
    even_y = even("gy")
    lane = lax.broadcasted_iota(jnp.int32, (8, 128), 1)
    slot = lane // 8
    firsthalf = lane % 8 < 3
    for f in range(3):
        packed = {}
        for d in range(16):
            source, base = source_rows(inside, border, f, d)
            whole, k = place_of(d)
            at = f * 16 + (k if whole else 10 + k)
            e = (f * 16 + d) * 48
            a = inner[pl.ds(at, 3, stride=48), :]
            b = outer[pl.ds(at, 3, stride=48), :]
            edge[e + 5 : e + 8, :] = jnp.where(even_x, b, a)
            edge[e + 8 : e + 24, :] = source[base : base + 16, :]
            edge[e + 24 : e + 40, :] = source[base + 48 : base + 64, :]
            edge[e + 40 : e + 43, :] = jnp.where(even_x, a, b)
            for r, first in ((0, e + 5), (7, e + 29)):
                v = [edge[first + k : first + k + 8, :] for k in range(7)]
                for g, value in filtered_columns(f, v):
                    row = g * 256 + d * 16 + (8 if r else 0)
                    out[row : row + 8, :] = value
                    packed[g, r] = collect(slot, packed.get((g, r), 0.0), d, value)
        for g in sorted({g for g, r in packed}):
            tiles = [packed[g, 0]]
            tiles += [edges[g * 48 + r * 8 : g * 48 + r * 8 + 8, :] for r in range(6)]
            tiles += [packed[g, 7]]
            for q in range(4):
                a, b = tiles[2 * q : 2 * q + 2]
                at = g * 32 + q * 8
                up = jnp.where(firsthalf, a, pltpu.roll(b, 3, 1))
                down = jnp.where(firsthalf, pltpu.roll(a, 125, 1), b)
                to_inner[at : at + 8, :] = jnp.where(even_y, up, down)
                to_outer[at : at + 8, :] = jnp.where(even_y, down, up)


def lanes_from(value, offset):
    return pltpu.roll(value, -offset % 128, 1)


def row_matrix():
    matrix = np.zeros((128, 256), np.float64)
    for j in range(128):
        for o in range(-3, 4):
            if 0 <= j + o < 128:
                matrix[j + o, j] = SMOOTH[o + 3]
                matrix[j + o, 128 + j] = SLOPE[o + 3]
    matrix = matrix.astype(np.float32)
    high = matrix.astype(jnp.bfloat16)
    low = (matrix - high.astype(np.float32)).astype(jnp.bfloat16)
    return np.concatenate([high, high, low, low], axis=0)


def row_kernel(middle, ends, matrix, out):
    def filtered(g, weights):
        rows = jnp.concatenate(
            [
                middle[pl.ds(pl.multiple_of(g * 768, 768), 768), :],
                ends[pl.ds(pl.multiple_of(g * 256, 256), 256), :],
            ],
            axis=0,
        )
        high = rows.astype(BF16)
        low = (rows - high.astype(F32)).astype(BF16)
        cells = jnp.concatenate([high, low, high, low], axis=1)
        return jnp.dot(cells, weights, preferred_element_type=F32)

    both = filtered(0, matrix[...])
    out[0:1024, :] = both[:, 0:128]
    out[4096:5120, :] = both[:, 128:256]

    def rest(g, carry):
        at = pl.ds(pl.multiple_of(g * 1024, 1024), 1024)
        out[at, :] = filtered(g, matrix[:, 0:128])
        return carry

    lax.fori_loop(1, 4, rest, 0)


def edge_matrix():
    matrix = np.zeros((256, 512), np.float32)
    for d in range(16):
        for h in range(2):
            for lane in range(6):
                for o in (-3, -2, -1, 1, 2, 3):
                    cell = lane + o
                    if 0 <= cell < 6 and (lane < 3) == (o > 0) and (lane < 3) != (cell < 3):
                        row = 8 * d + 3 * h + cell % 3 + (128 if cell >= 3 else 0)
                        column = 256 * h + 8 * d + lane
                        matrix[row, column] = SMOOTH[o + 3]
                        matrix[row, column + 128] = SLOPE[o + 3]
    return matrix


def place_matrix():
    matrix = np.zeros((256, 2048), np.float32)
    for d in range(16):
        for lane in range(6):
            matrix[8 * d + lane, d * 128 + (lane + 125) % 128] = 1.0
            matrix[128 + 8 * d + lane, d * 128 + (lane + 125) % 128] = 1.0
    return matrix.astype(jnp.bfloat16)


def sample_kernel(
    light, source, inner, outer, matrix, places, transfer, out, grids, *, scale
):
    even_y = even("gy")
    lane = lax.broadcasted_iota(jnp.int32, (8, 128), 1)
    left = jnp.where(even_y, outer[...], inner[...])
    right = jnp.where(even_y, inner[...], outer[...])
    terms = jnp.dot(
        jnp.concatenate([left, right], axis=1),
        matrix[...],
        precision=lax.Precision.HIGHEST,
        preferred_element_type=F32,
    )
    packed = jnp.concatenate(
        [
            terms[(g % 4) * 32 + (r // 2) * 8 :][:8, (r % 2) * 256 + (128 if g == 4 else 0) :][:, :128]
            for g in range(5)
            for r in range(8)
        ],
        axis=0,
    )
    high = packed.astype(BF16)
    low = (packed - high.astype(F32)).astype(BF16)
    packed = jnp.concatenate([high, low], axis=1)
    for pair in range(8):
        moved = jnp.dot(
            packed, places[:, pair * 256 : pair * 256 + 256], preferred_element_type=F32
        )
        for g in range(5):
            for r in range(8):
                for h in range(2):
                    d = pair * 2 + h
                    at = g * 1024 + d * 64 + r * 8
                    inside = 0 < r < 7
                    row = g * 1024 + (d * 48 + r * 8 - 8 if inside else 768 + d * 16 + r // 7 * 8)
                    grids[at : at + 8, :] = (
                        source[row : row + 8, :]
                        + moved[g * 64 + r * 8 : g * 64 + r * 8 + 8, h * 128 : h * 128 + 128]
                    )

    bins = 128
    step = 3.0 / 32760.0
    table = []
    for c in range(4):
        entry = jnp.round(jnp.broadcast_to(transfer[c : c + 1, :], (8, bins)) * (1.0 / step))
        rise = jnp.where(lane < bins - 1, lanes_from(entry, 1) - entry, 0.0)
        table.append(entry.astype(jnp.int32) * 65536 + (rise.astype(jnp.int32) & 65535))
    light_x, light_y, light_z = light[0:8, :], light[8:16, :], light[16:24, :]
    def tile(r, carry):
        total = [jnp.zeros((8, 128), F32)] * 3
        through = jnp.ones((8, 128), F32)
        for d in range(16):
            at = pl.multiple_of(d * 64 + r * 8, 8)
            value, grad_x, grad_z, mixture, grad_y = [
                grids[pl.ds(g * 1024 + at, 8), :] for g in range(5)
            ]
            position = jax.nn.sigmoid(value) * (bins - 1)
            whole = jnp.floor(position)
            part = position - whole
            index = whole.astype(jnp.int32)
            looked = []
            for c in range(4):
                both = jnp.take_along_axis(table[c], index, axis=1, mode="promise_in_bounds")
                entry = lax.shift_right_arithmetic(both, 16).astype(F32)
                rise = lax.shift_right_arithmetic(lax.shift_left(both, 16), 16).astype(F32)
                looked.append(entry + part * rise)
            facing = grad_x * light_x + grad_y * light_y + grad_z * light_z
            diffuse = (
                facing
                * facing
                / (grad_x * grad_x + grad_y * grad_y + grad_z * grad_z + SHADE_FLOOR)
            )
            shade = 0.25 + 0.75 * diffuse
            alpha = 1.0 - jnp.exp(scale * step * looked[3] * jax.nn.sigmoid(mixture))
            covered = through * alpha
            shaded = covered * shade
            for c in range(3):
                total[c] = total[c] + shaded * looked[c]
            through = through - covered
        at = pl.multiple_of(r * 32, 32)
        for c in range(3):
            out[pl.ds(at + c * 8, 8), :] = total[c] * step
        out[pl.ds(at + 24, 8), :] = 1.0 - through
        return carry

    lax.fori_loop(0, 8, tile, 0)


def over_kernel(pieces, out):
    total = [pieces[pl.ds(c * 8, 8), :] for c in range(4)]
    for k in range(1, 8):
        through = 1.0 - total[3]
        for c in range(4):
            total[c] = total[c] + through * pieces[pl.ds(k * 32 + c * 8, 8), :]
    for c in range(4):
        out[pl.ds(c * 8, 8), :] = total[c]


VMEM = pl.BlockSpec(memory_space=pltpu.VMEM)
SMEM = pl.BlockSpec(memory_space=pltpu.SMEM)
HBM = pl.BlockSpec(memory_space=pltpu.HBM)


def call(kernel, name, args, outs, scratch=(), spaces=None, targets=None, limit=16 * 2**20):
    return pl.pallas_call(
        kernel,
        name=name,
        out_shape=[jax.ShapeDtypeStruct(shape, F32) for shape in outs],
        in_specs=spaces or [VMEM] * len(args),
        out_specs=targets or [VMEM] * len(outs),
        scratch_shapes=scratch,
        compiler_params=pltpu.CompilerParams(vmem_limit_bytes=limit),
    )(*args)


def swap(inner, outer, axis):
    size = lax.axis_size(axis)
    lines = 1 if axis == "gy" else lax.axis_size("gy")
    exchanges = ([], [])
    for line in range(lines):
        for i in range(size):
            for turn in range(2):
                other = i + 1 if (i + line + turn) % 2 == 0 else i - 1
                if 0 <= other < size:
                    pair = (i, other)
                    if axis == "gz":
                        pair = (line * size + i, line * size + other)
                    if axis == "gx":
                        pair = (i * lines + line, other * lines + line)
                    exchanges[turn].append(pair)
    axes = {"gx": ("gx", "gy"), "gy": "gy", "gz": ("gy", "gz")}[axis]
    return lax.ppermute(inner, axes, exchanges[0]), lax.ppermute(outer, axes, exchanges[1])


def even(axis):
    line = 0 if axis == "gy" else lax.axis_index("gy")
    return (lax.axis_index(axis) + line) % 2 == 0


def shards(field, transfer, light_angles):
    depth_count = lax.axis_size("gz")
    depth_step = 1.0 / (field.shape[1] * depth_count)
    field = field.reshape(2048, 128)
    faces = call(
        faces_kernel,
        "faces",
        (field,),
        ((384, 128), (384, 128)),
        [pltpu.SemaphoreType.DMA((4,))],
        [HBM],
        None,
        55800000,
    )
    inner, outer = swap(*faces, "gz")
    inside, light = call(
        inside_kernel, "inside", (light_angles, field), ((1920, 128), (24, 128)), (), [SMEM, VMEM]
    )
    to_inner, to_outer = call(
        cross_faces_kernel,
        "cross_faces",
        (field, inside, inner, outer),
        ((144, 128), (144, 128)),
        [pltpu.VMEM((288, 128), F32)],
    )
    (border,) = call(border_kernel, "border", (field, inner, outer), ((1152, 128),))
    inner, outer = swap(to_inner, to_outer, "gx")
    middle, edges = call(middle_kernel, "middle", (inside, border), ((3072, 128), (192, 128)))
    ends, to_inner, to_outer = call(
        ends_kernel,
        "ends",
        (inside, border, edges, inner, outer),
        ((1024, 128), (128, 128), (128, 128)),
        [pltpu.VMEM((2304, 128), F32)],
    )
    inner, outer = swap(to_inner, to_outer, "gy")
    (rows,) = call(row_kernel, "rows", (middle, ends, jnp.asarray(row_matrix())), ((5120, 128),))
    (partial_value,) = call(
        functools.partial(sample_kernel, scale=-OPTICAL * depth_step),
        "sample",
        (
            light,
            rows,
            inner,
            outer,
            jnp.asarray(edge_matrix()),
            jnp.asarray(place_matrix()),
            transfer,
        ),
        ((256, 128),),
        [pltpu.VMEM((5120, 128), F32)],
    )
    pieces = lax.all_to_all(partial_value.reshape(8, 32, 128), "gz", 0, 0)
    (image,) = call(over_kernel, "over", (pieces.reshape(256, 128),), ((32, 128),))
    return image.reshape(4, 8, 128)


def solution(mesh):
    placed = (P(None, "gz", "gx", "gy"), P(), P())
    return jax.shard_map(
        shards, mesh=mesh, in_specs=placed, out_specs=P(None, ("gx", "gz"), "gy"), check_vma=False
    )
```

```python
import functools
import math

import jax
import jax.numpy as jnp
import numpy as np
from jax import lax
from jax.experimental import pallas as pl
from jax.experimental.pallas import tpu as pltpu
from jax.sharding import PartitionSpec as P

SIGMA_TAPS = 1.2
OPTICAL = 2.0
SHADE_FLOOR = 0.25
F32 = jnp.float32
BF16 = jnp.bfloat16


def filter_taps():
    places = [-3, -2, -1, 0, 1, 2, 3]
    bell = [math.exp(-place * place / (2.0 * SIGMA_TAPS * SIGMA_TAPS)) for place in places]
    bell_total = sum(bell)
    slope_total = sum((place * place * weight for place, weight in zip(places, bell)))
    smooth_taps = [weight / bell_total for weight in bell]
    slope_taps = [place * weight / slope_total for place, weight in zip(places, bell)]
    return (smooth_taps, slope_taps)


SMOOTH, SLOPE = filter_taps()


def smooth7(v):
    return (
        SMOOTH[3] * v[3]
        + SMOOTH[4] * (v[2] + v[4])
        + SMOOTH[5] * (v[1] + v[5])
        + SMOOTH[6] * (v[0] + v[6])
    )


def slope7(v):
    return SLOPE[4] * (v[4] - v[2]) + SLOPE[5] * (v[5] - v[1]) + SLOPE[6] * (v[6] - v[0])


INSIDE = list(range(3, 13))
BORDER = [0, 1, 2, 13, 14, 15]


def place_of(d):
    return (True, d - 3) if 3 <= d <= 12 else (False, BORDER.index(d))


def faces_kernel(field, to_inner, to_outer, done):
    high = pl.multiple_of(jnp.where(even("gz"), 832, 0), 64)
    copies = []
    for k, (target, first) in enumerate(((to_inner, high), (to_outer, 832 - high))):
        for f in range(2):
            rows = pl.ds(pl.multiple_of(f * 1024 + first, 64), 192)
            copies.append(
                pltpu.make_async_copy(
                    field.at[rows, :], target.at[pl.ds(f * 192, 192), :], done.at[2 * k + f]
                )
            )
    for copy in copies:
        copy.start()
    for copy in copies:
        copy.wait()


def inside_kernel(angles, field, out, light):
    azimuth = jnp.full((8, 128), angles[0])
    polar = jnp.full((8, 128), angles[1])
    light[0:8, :] = jnp.cos(azimuth) * jnp.sin(polar)
    light[8:16, :] = jnp.sin(azimuth) * jnp.sin(polar)
    light[16:24, :] = jnp.cos(polar)

    def tile(r, carry):
        at = pl.multiple_of(r * 8, 8)
        first = [field[pl.ds(d * 64 + at, 8), :] for d in range(16)]
        second = [field[pl.ds(1024 + d * 64 + at, 8), :] for d in range(16)]
        for k in range(10):
            out[pl.ds(k * 64 + at, 8), :] = smooth7(first[k : k + 7])
            out[pl.ds(640 + k * 64 + at, 8), :] = slope7(first[k : k + 7])
            out[pl.ds(1280 + k * 64 + at, 8), :] = smooth7(second[k : k + 7])
        return carry

    lax.fori_loop(0, 8, tile, 0)


def border_rows(field, inner, outer, out, at, to):
    even_z = even("gz")

    def plane(f, d):
        if d < 0:
            rows = pl.ds(f * 192 + (d + 3) * 64 + at, 8)
            return jnp.where(even_z, outer[rows, :], inner[rows, :])
        if d > 15:
            rows = pl.ds(f * 192 + (d - 16) * 64 + at, 8)
            return jnp.where(even_z, inner[rows, :], outer[rows, :])
        return field[pl.ds(f * 1024 + d * 64 + at, 8), :]

    stride = out.shape[0] // 18
    for half in range(2):
        start = 13 * half
        first = [plane(0, d) for d in range(start - 3, start + 6)]
        second = [plane(1, d) for d in range(start - 3, start + 6)]
        for k in range(3):
            row = (half * 3 + k) * stride + to
            out[pl.ds(row, 8), :] = smooth7(first[k : k + 7])
            out[pl.ds(6 * stride + row, 8), :] = slope7(first[k : k + 7])
            out[pl.ds(12 * stride + row, 8), :] = smooth7(second[k : k + 7])


def cross_faces_kernel(field, inside, inner, outer, to_inner, to_outer, ends):
    even_x = even("gx")
    border_rows(field, inner, outer, ends, 0, 0)
    border_rows(field, inner, outer, ends, 56, 8)
    for j in range(3):
        for f in range(3):
            at = j * 48 + f * 16
            for source, planes, first, size in ((inside, 10, at, 64), (ends, 6, at + 10, 16)):
                base = f * planes * size + j
                low = source[pl.ds(base, planes, stride=size), :]
                high = source[pl.ds(base + size - 3, planes, stride=size), :]
                to_inner[pl.ds(first, planes), :] = jnp.where(even_x, high, low)
                to_outer[pl.ds(first, planes), :] = jnp.where(even_x, low, high)


def border_kernel(field, inner, outer, out):
    def tile(r, carry):
        at = pl.multiple_of(r * 8, 8)
        border_rows(field, inner, outer, out, at, at)
        return carry

    lax.fori_loop(0, 8, tile, 0)


def source_rows(inside, border, f, d):
    inner, k = place_of(d)
    return (inside, (f * 10 + k) * 64) if inner else (border, (f * 6 + k) * 64)


def collect(slot, packed, d, value):
    return jnp.where(slot == d, pltpu.roll(value, (8 * d + 3) % 128, 1), packed)


def filtered_columns(f, v):
    return [(0, smooth7(v)), (1, slope7(v))] if f == 0 else [(f + 1, smooth7(v))]


def middle_kernel(inside, border, out, edges):
    slot = lax.broadcasted_iota(jnp.int32, (8, 128), 1) // 8
    for f in range(3):
        packed = {}
        for d in range(16):
            source, base = source_rows(inside, border, f, d)
            for r in range(1, 7):
                first = base + r * 8 - 3
                v = [source[first + k : first + k + 8, :] for k in range(7)]
                for g, value in filtered_columns(f, v):
                    row = g * 768 + d * 48 + (r - 1) * 8
                    out[row : row + 8, :] = value
                    packed[g, r] = collect(slot, packed.get((g, r), 0.0), d, value)
        for (g, r), value in packed.items():
            edges[g * 48 + (r - 1) * 8 : g * 48 + r * 8, :] = value


def ends_kernel(inside, border, edges, inner, outer, out, to_inner, to_outer, edge):
    even_x = even("gx")
    even_y = even("gy")
    lane = lax.broadcasted_iota(jnp.int32, (8, 128), 1)
    slot = lane // 8
    firsthalf = lane % 8 < 3
    for f in range(3):
        packed = {}
        for d in range(16):
            source, base = source_rows(inside, border, f, d)
            whole, k = place_of(d)
            at = f * 16 + (k if whole else 10 + k)
            e = (f * 16 + d) * 48
            a = inner[pl.ds(at, 3, stride=48), :]
            b = outer[pl.ds(at, 3, stride=48), :]
            edge[e + 5 : e + 8, :] = jnp.where(even_x, b, a)
            edge[e + 8 : e + 24, :] = source[base : base + 16, :]
            edge[e + 24 : e + 40, :] = source[base + 48 : base + 64, :]
            edge[e + 40 : e + 43, :] = jnp.where(even_x, a, b)
            for r, first in ((0, e + 5), (7, e + 29)):
                v = [edge[first + k : first + k + 8, :] for k in range(7)]
                for g, value in filtered_columns(f, v):
                    row = g * 256 + d * 16 + (8 if r else 0)
                    out[row : row + 8, :] = value
                    packed[g, r] = collect(slot, packed.get((g, r), 0.0), d, value)
        for g in sorted({g for g, r in packed}):
            tiles = [packed[g, 0]]
            tiles += [edges[g * 48 + r * 8 : g * 48 + r * 8 + 8, :] for r in range(6)]
            tiles += [packed[g, 7]]
            for q in range(4):
                a, b = tiles[2 * q : 2 * q + 2]
                at = g * 32 + q * 8
                up = jnp.where(firsthalf, a, pltpu.roll(b, 3, 1))
                down = jnp.where(firsthalf, pltpu.roll(a, 125, 1), b)
                to_inner[at : at + 8, :] = jnp.where(even_y, up, down)
                to_outer[at : at + 8, :] = jnp.where(even_y, down, up)


def lanes_from(value, offset):
    return pltpu.roll(value, -offset % 128, 1)


def row_matrix():
    matrix = np.zeros((128, 256), np.float64)
    for j in range(128):
        for o in range(-3, 4):
            if 0 <= j + o < 128:
                matrix[j + o, j] = SMOOTH[o + 3]
                matrix[j + o, 128 + j] = SLOPE[o + 3]
    matrix = matrix.astype(np.float32)
    high = matrix.astype(jnp.bfloat16)
    low = (matrix - high.astype(np.float32)).astype(jnp.bfloat16)
    return np.concatenate([high, high, low, low], axis=0)


def row_kernel(middle, ends, matrix, out):
    def filtered(g, weights):
        rows = jnp.concatenate(
            [
                middle[pl.ds(pl.multiple_of(g * 768, 768), 768), :],
                ends[pl.ds(pl.multiple_of(g * 256, 256), 256), :],
            ],
            axis=0,
        )
        high = rows.astype(BF16)
        low = (rows - high.astype(F32)).astype(BF16)
        cells = jnp.concatenate([high, low, high, low], axis=1)
        return jnp.dot(cells, weights, preferred_element_type=F32)

    both = filtered(0, matrix[...])
    out[0:1024, :] = both[:, 0:128]
    out[4096:5120, :] = both[:, 128:256]

    def rest(g, carry):
        at = pl.ds(pl.multiple_of(g * 1024, 1024), 1024)
        out[at, :] = filtered(g, matrix[:, 0:128])
        return carry

    lax.fori_loop(1, 4, rest, 0)


def edge_matrix():
    matrix = np.zeros((256, 512), np.float32)
    for d in range(16):
        for h in range(2):
            for lane in range(6):
                for o in (-3, -2, -1, 1, 2, 3):
                    cell = lane + o
                    if 0 <= cell < 6 and (lane < 3) == (o > 0) and (lane < 3) != (cell < 3):
                        row = 8 * d + 3 * h + cell % 3 + (128 if cell >= 3 else 0)
                        column = 256 * h + 8 * d + lane
                        matrix[row, column] = SMOOTH[o + 3]
                        matrix[row, column + 128] = SLOPE[o + 3]
    return matrix


def place_matrix():
    matrix = np.zeros((256, 2048), np.float32)
    for d in range(16):
        for lane in range(6):
            matrix[8 * d + lane, d * 128 + (lane + 125) % 128] = 1.0
            matrix[128 + 8 * d + lane, d * 128 + (lane + 125) % 128] = 1.0
    return matrix.astype(jnp.bfloat16)


def sample_kernel(
    light, source, inner, outer, matrix, places, transfer, out, grids, *, scale
):
    even_y = even("gy")
    lane = lax.broadcasted_iota(jnp.int32, (8, 128), 1)
    left = jnp.where(even_y, outer[...], inner[...])
    right = jnp.where(even_y, inner[...], outer[...])
    terms = jnp.dot(
        jnp.concatenate([left, right], axis=1),
        matrix[...],
        precision=lax.Precision.HIGHEST,
        preferred_element_type=F32,
    )
    packed = jnp.concatenate(
        [
            terms[(g % 4) * 32 + (r // 2) * 8 :][:8, (r % 2) * 256 + (128 if g == 4 else 0) :][:, :128]
            for g in range(5)
            for r in range(8)
        ],
        axis=0,
    )
    high = packed.astype(BF16)
    low = (packed - high.astype(F32)).astype(BF16)
    packed = jnp.concatenate([high, low], axis=1)
    for pair in range(8):
        moved = jnp.dot(
            packed, places[:, pair * 256 : pair * 256 + 256], preferred_element_type=F32
        )
        for g in range(5):
            for r in range(8):
                for h in range(2):
                    d = pair * 2 + h
                    at = g * 1024 + d * 64 + r * 8
                    inside = 0 < r < 7
                    row = g * 1024 + (d * 48 + r * 8 - 8 if inside else 768 + d * 16 + r // 7 * 8)
                    grids[at : at + 8, :] = (
                        source[row : row + 8, :]
                        + moved[g * 64 + r * 8 : g * 64 + r * 8 + 8, h * 128 : h * 128 + 128]
                    )

    bins = 128
    step = 3.0 / 32760.0
    table = []
    for c in range(4):
        entry = jnp.round(jnp.broadcast_to(transfer[c : c + 1, :], (8, bins)) * (1.0 / step))
        rise = jnp.where(lane < bins - 1, lanes_from(entry, 1) - entry, 0.0)
        table.append(entry.astype(jnp.int32) * 65536 + (rise.astype(jnp.int32) & 65535))
    light_x, light_y, light_z = light[0:8, :], light[8:16, :], light[16:24, :]
    def tile(r, carry):
        total = [jnp.zeros((8, 128), F32)] * 3
        through = jnp.ones((8, 128), F32)
        for d in range(16):
            at = pl.multiple_of(d * 64 + r * 8, 8)
            value, grad_x, grad_z, mixture, grad_y = [
                grids[pl.ds(g * 1024 + at, 8), :] for g in range(5)
            ]
            position = jax.nn.sigmoid(value) * (bins - 1)
            whole = jnp.floor(position)
            part = position - whole
            index = whole.astype(jnp.int32)
            looked = []
            for c in range(4):
                both = jnp.take_along_axis(table[c], index, axis=1, mode="promise_in_bounds")
                entry = lax.shift_right_arithmetic(both, 16).astype(F32)
                rise = lax.shift_right_arithmetic(lax.shift_left(both, 16), 16).astype(F32)
                looked.append(entry + part * rise)
            facing = grad_x * light_x + grad_y * light_y + grad_z * light_z
            diffuse = (
                facing
                * facing
                / (grad_x * grad_x + grad_y * grad_y + grad_z * grad_z + SHADE_FLOOR)
            )
            shade = 0.25 + 0.75 * diffuse
            alpha = 1.0 - jnp.exp(scale * step * looked[3] * jax.nn.sigmoid(mixture))
            covered = through * alpha
            shaded = covered * shade
            for c in range(3):
                total[c] = total[c] + shaded * looked[c]
            through = through - covered
        at = pl.multiple_of(r * 32, 32)
        for c in range(3):
            out[pl.ds(at + c * 8, 8), :] = total[c] * step
        out[pl.ds(at + 24, 8), :] = 1.0 - through
        return carry

    lax.fori_loop(0, 8, tile, 0)


def over_kernel(pieces, out):
    total = [pieces[pl.ds(c * 8, 8), :] for c in range(4)]
    for k in range(1, 8):
        through = 1.0 - total[3]
        for c in range(4):
            total[c] = total[c] + through * pieces[pl.ds(k * 32 + c * 8, 8), :]
    for c in range(4):
        out[pl.ds(c * 8, 8), :] = total[c]


VMEM = pl.BlockSpec(memory_space=pltpu.VMEM)
SMEM = pl.BlockSpec(memory_space=pltpu.SMEM)
HBM = pl.BlockSpec(memory_space=pltpu.HBM)


def call(kernel, name, args, outs, scratch=(), spaces=None, targets=None, limit=16 * 2**20):
    return pl.pallas_call(
        kernel,
        name=name,
        out_shape=[jax.ShapeDtypeStruct(shape, F32) for shape in outs],
        in_specs=spaces or [VMEM] * len(args),
        out_specs=targets or [VMEM] * len(outs),
        scratch_shapes=scratch,
        compiler_params=pltpu.CompilerParams(vmem_limit_bytes=limit),
    )(*args)


def swap(inner, outer, axis):
    size = lax.axis_size(axis)
    lines = 1 if axis == "gy" else lax.axis_size("gy")
    exchanges = ([], [])
    for line in range(lines):
        for i in range(size):
            for turn in range(2):
                first = line + 1 if axis == "gy" else line
                other = i + 1 if (i + first + turn) % 2 == 0 else i - 1
                if 0 <= other < size:
                    pair = (i, other)
                    if axis == "gz":
                        pair = (line * size + i, line * size + other)
                    if axis == "gx":
                        pair = (i * lines + line, other * lines + line)
                    exchanges[turn].append(pair)
    axes = {"gx": ("gx", "gy"), "gy": "gy", "gz": ("gy", "gz")}[axis]
    return lax.ppermute(inner, axes, exchanges[0]), lax.ppermute(outer, axes, exchanges[1])


def even(axis):
    line = 1 if axis == "gy" else lax.axis_index("gy")
    return (lax.axis_index(axis) + line) % 2 == 0


def shards(field, transfer, light_angles):
    depth_count = lax.axis_size("gz")
    depth_step = 1.0 / (field.shape[1] * depth_count)
    field = field.reshape(2048, 128)
    faces = call(
        faces_kernel,
        "faces",
        (field,),
        ((384, 128), (384, 128)),
        [pltpu.SemaphoreType.DMA((4,))],
        [HBM],
        None,
        55800000,
    )
    inner, outer = swap(*faces, "gz")
    inside, light = call(
        inside_kernel, "inside", (light_angles, field), ((1920, 128), (24, 128)), (), [SMEM, VMEM]
    )
    to_inner, to_outer = call(
        cross_faces_kernel,
        "cross_faces",
        (field, inside, inner, outer),
        ((144, 128), (144, 128)),
        [pltpu.VMEM((288, 128), F32)],
    )
    (border,) = call(border_kernel, "border", (field, inner, outer), ((1152, 128),))
    inner, outer = swap(to_inner, to_outer, "gx")
    middle, edges = call(middle_kernel, "middle", (inside, border), ((3072, 128), (192, 128)))
    ends, to_inner, to_outer = call(
        ends_kernel,
        "ends",
        (inside, border, edges, inner, outer),
        ((1024, 128), (128, 128), (128, 128)),
        [pltpu.VMEM((2304, 128), F32)],
    )
    inner, outer = swap(to_inner, to_outer, "gy")
    (rows,) = call(row_kernel, "rows", (middle, ends, jnp.asarray(row_matrix())), ((5120, 128),))
    (partial_value,) = call(
        functools.partial(sample_kernel, scale=-OPTICAL * depth_step),
        "sample",
        (
            light,
            rows,
            inner,
            outer,
            jnp.asarray(edge_matrix()),
            jnp.asarray(place_matrix()),
            transfer,
        ),
        ((256, 128),),
        [pltpu.VMEM((5120, 128), F32)],
    )
    pieces = lax.all_to_all(partial_value.reshape(8, 32, 128), "gz", 0, 0)
    (image,) = call(over_kernel, "over", (pieces.reshape(256, 128),), ((32, 128),))
    return image.reshape(4, 8, 128)


def solution(mesh):
    placed = (P(None, "gz", "gx", "gy"), P(), P())
    return jax.shard_map(
        shards, mesh=mesh, in_specs=placed, out_specs=P(None, ("gx", "gz"), "gy"), check_vma=False
    )
```
